32 devices in a mesh: job: 2 (over y), pole: 4 (over z), col: 4 (over x, core).
Axes of the slice: x: 2, y: 2, z: 4, core: 2. Of those that a mesh axis runs over, the one named last changes fastest.
Arguments:
- inverse: bfloat16 [8, 2, 6144, 6144], P(('job', 'pole'), None, 'col'), parts along dimension 0, may hold values from -6 to 6
- panels: bfloat16 [8, 3, 2, 6144, 128], P(('job', 'pole'), None, None, 'col'), parts along dimension 0, may hold values from -0.078125 to 0.078125
- diag_inverse: float32 [8, 3, 2, 128, 128], P(('job', 'pole')), parts along dimension 0, may hold values from -6 to 6
- pole_weights: float32 [8, 2], P(('job', 'pole')), parts along dimension 0, may hold values from -1 to 1
- supports: int32 [32, 8], replicated, may hold values from 0 to 143, as said below
- counts: int32 [32], replicated, may hold values from 1 to 8, as said below
- panel_order: int32 [3], replicated, may hold values from 0 to 2, each once
- row_orbitals: bfloat16 [64, 8, 128, 512], P(('job', 'col'), None, None, 'pole'), parts along dimension 0, may hold values from -0.5 to 0.5
- panel_orbitals: bfloat16 [64, 3, 128, 512], P(('job', 'col'), None, None, 'pole'), parts along dimension 0, may hold values from -0.078125 to 0.078125
- core_density: float32 [64, 512], P(('job', 'col'), 'pole'), parts along dimension 0, may hold values from 0.5 to 4
Outputs:
- valence_density: float32 [64, 512], P(('job', 'col'), 'pole'), parts along dimension 0
- exchange_potential: float32 [64, 512], P(('job', 'col'), 'pole'), parts along dimension 0
- diag_density: float32 [6, 128, 128], P('job'), parts along dimension 0
The draws below stay inside these ranges and needn't reach their ends.
There are 2 independent parts, one for each index of `job`. The reference program is written for one: setup_inputs(seed, part) draws one part's arguments, and reference() takes and returns one part's arrays. A program takes and returns all parts, laid end to end along the dimension named above; an argument that names none is the same for every part. Nothing has to cross between parts.
Inputs may be any that keep to these rules, and one draw needn't show every extreme that they name: `supports`: the ids within one tile's list are distinct. Block g belongs to index g // 36 of col. Over the first counts[t] entries of all tiles of one index of col, at most 3 distinct blocks belong to any one index of col, and exactly 3 for some pair in every draw. `counts`: some tile of every index of col has a full list.
All inputs are finite; a program needn't handle non-finite values.
Results may differ from the reference program's by a relative error of at most 0.0029.
Values may be sent and summed in bfloat16 or wider, within the bound.
No kernel may reach another device: no remote copies, remote signals or barrier semaphores. Data moves between devices by JAX's collectives and lax.ppermute only.
A program may use at most 128 MiB of HBM per device.

```python
import math
import jax
import jax.numpy as jnp
from jax import lax

M = 6144
W = 128
PANELS = 3
TILE_DEV = 8
S_MAX = 8
CAP = 3
POLES = 4
TILES = 32
R = 512
NB = 144
B_DEV = 36


def support_tables(key):
    base = jax.random.fold_in(key, 4099)
    first_key, second_key, third_key = jax.random.split(base, 3)
    col_count = TILES // TILE_DEV
    pool_size = col_count * CAP
    ranking = jax.random.randint(first_key, (col_count, col_count, B_DEV), 0, 1 << 20) * B_DEV + jnp.arange(B_DEV, dtype=jnp.int32)
    allowed = jnp.argsort(ranking, axis=-1)[:, :, :CAP].astype(jnp.int32)
    tile_ids = jnp.arange(TILES, dtype=jnp.int32)
    owner_dest = tile_ids // TILE_DEV
    item_ids = jnp.arange(pool_size, dtype=jnp.int32)
    source_of = item_ids // CAP
    forced = (tile_ids % TILE_DEV == 0)[:, None] & (source_of[None, :] == ((owner_dest + 1) % col_count)[:, None])
    scores = jax.random.randint(second_key, (TILES, pool_size), 0, 1 << 20) * pool_size + item_ids[None, :] + pool_size
    scores = jnp.where(forced, item_ids[None, :], scores)
    picked_items = jnp.argsort(scores, axis=1)[:, :S_MAX].astype(jnp.int32)
    sources = picked_items // CAP
    ranks = picked_items % CAP
    local_pick = allowed[owner_dest[:, None], sources, ranks]
    support_ids = (sources * B_DEV + local_pick).astype(jnp.int32)
    lengths = jax.random.randint(third_key, (TILES,), 1, S_MAX + 1)
    lengths = jnp.where(tile_ids % TILE_DEV == 0, S_MAX, lengths).astype(jnp.int32)
    return (support_ids, lengths)


def draw_supports(key, part):
    return support_tables(key)[0]


def draw_counts(key, part):
    return support_tables(key)[1]


def block_scale(rng, shape, cuts, low, high):
    def one(axis_at, shards_of):
        draws = jax.random.uniform(jax.random.fold_in(jax.random.fold_in(rng, 6), axis_at), (shards_of,), jnp.float32, low / len(cuts), high / len(cuts))
        return jnp.repeat(jnp.exp(draws), shape[axis_at] // shards_of).reshape((-1,) + (1,) * (len(shape) - axis_at - 1))

    level = one(*cuts[0])
    for cut in cuts[1:]:
        level = level * one(*cut)
    return level


def normal_values(rng, shape, scale, reach, cuts=(), kind=jnp.bfloat16):
    drawn = jax.random.normal(rng, shape, jnp.float32) * scale
    if len(cuts) > 0:
        drawn = block_scale(rng, shape, cuts, -0.22, 0.18) * drawn
    return jnp.clip(drawn, min=-reach, max=reach).astype(kind)


def setup_inputs(seed: int = 0, part: int = 0) -> dict:
    keys = jax.random.split(jax.random.key(seed), 11)
    part_splits = jax.random.split(jax.random.fold_in(keys[10], part), 11)
    inverse = normal_values(part_splits[0], (POLES, 2, M, M), 1.0, 6.0, ((0, 4), (2, 4)))
    panels = normal_values(part_splits[1], (POLES, PANELS, 2, M, W), M ** -0.5, 0.078125, ((0, 4), (3, 4)))
    diag_inverse = normal_values(part_splits[2], (POLES, PANELS, 2, W, W), 1.0, 6.0, ((0, 4),), jnp.float32)
    pole_weights = jnp.clip(jax.random.uniform(part_splits[3], (POLES, 2), jnp.float32, -1.0, 1.0) * block_scale(part_splits[3], (POLES, 2), ((0, 4),), -0.4, 0.0), -1.0, 1.0)
    supports = draw_supports(jax.random.fold_in(keys[10], 71), part)
    counts = draw_counts(jax.random.fold_in(keys[10], 71), part)
    panel_order = jax.random.permutation(keys[6], PANELS).astype(jnp.int32)
    row_orbitals = normal_values(part_splits[7], (TILES, S_MAX, W, R), W ** -0.5, 0.5, ((0, 4), (3, 4)))
    panel_orbitals = normal_values(part_splits[8], (TILES, PANELS, W, R), (W * 48) ** -0.5, 0.078125, ((0, 4), (3, 4)))
    core_density = jnp.clip(jnp.exp(math.log(4.0) - 2.0794415 * jax.random.uniform(part_splits[9], (TILES, R), jnp.float32) ** block_scale(part_splits[9], (TILES, R), ((0, 4), (1, 4)), -0.2, 0.2)), 0.5, 4.0)
    return {"inverse": inverse, "panels": panels, "diag_inverse": diag_inverse, "pole_weights": pole_weights, "supports": supports, "counts": counts, "panel_order": panel_order, "row_orbitals": row_orbitals, "panel_orbitals": panel_orbitals, "core_density": core_density}


exchange_coeff = (3.0 / 3.141592653589793) ** (1.0 / 3.0)
density_floor = 0.5


def reference(inverse, panels, diag_inverse, pole_weights, supports, counts, panel_order, row_orbitals, panel_orbitals, core_density):
    order_list = panel_order

    def scan_step(carry, items):
        inverse_pole, panels_pole, diag_pole, weight = items
        ordered = jnp.take(panels_pole, order_list, axis=0)
        diag_ordered = jnp.take(diag_pole, order_list, axis=0)
        stacked = inverse_pole.reshape(2 * M, M)
        right_side = ordered.transpose(2, 0, 1, 3).reshape(M, PANELS * 2 * W)
        product = jnp.dot(stacked, right_side, preferred_element_type=jnp.float32).reshape(2, M, PANELS, 2, W)
        real_part = -(product[0, :, :, 0] - product[1, :, :, 1])
        imag_part = -(product[0, :, :, 1] + product[1, :, :, 0])
        density = weight[0] * imag_part + weight[1] * real_part
        lower_rows = ordered.astype(jnp.float32)
        highest = lax.Precision.HIGHEST
        cross_real = jnp.einsum("jiw,ijv->jwv", lower_rows[:, 0], real_part, precision=highest) - jnp.einsum("jiw,ijv->jwv", lower_rows[:, 1], imag_part, precision=highest)
        cross_imag = jnp.einsum("jiw,ijv->jwv", lower_rows[:, 0], imag_part, precision=highest) + jnp.einsum("jiw,ijv->jwv", lower_rows[:, 1], real_part, precision=highest)
        diag_term = weight[0] * (diag_ordered[:, 1] - cross_imag) + weight[1] * (diag_ordered[:, 0] - cross_real)
        return (carry[0] + density, carry[1] + diag_term), None

    start = (jnp.zeros((M, PANELS, W), jnp.float32), jnp.zeros((PANELS, W, W), jnp.float32))
    (density, diag_density), unused = lax.scan(scan_step, start, (inverse, panels, diag_inverse, pole_weights))
    density_blocks = density.astype(jnp.bfloat16)
    blocks = density_blocks.reshape(M // W, W, PANELS, W).transpose(0, 2, 1, 3).reshape(NB, W, W)

    def tile_step(items):
        support, count, orbitals, panel_values, core = items
        picked = blocks[support].astype(jnp.float32)
        chosen = panel_values[support % PANELS].astype(jnp.float32)
        mixed = jnp.einsum("kim,kmr->kir", picked, chosen)
        contribution = jnp.sum(orbitals.astype(jnp.float32) * mixed, axis=1)
        live_slots = (jnp.arange(S_MAX, dtype=jnp.int32) < count).astype(jnp.float32)
        valence = jnp.sum(contribution * live_slots[:, None], axis=0)
        clamped = jnp.maximum(core + valence, density_floor)
        return valence, -exchange_coeff * clamped ** (1.0 / 3.0)

    valence_density, exchange_potential = lax.map(tile_step, (supports, counts, row_orbitals, panel_orbitals, core_density))
    return valence_density, exchange_potential, diag_density
```

```python
import functools

import jax
import jax.numpy as jnp
from jax import lax
from jax.experimental import pallas as pl
from jax.experimental.pallas import tpu as pltpu
from jax.sharding import PartitionSpec as P

CAP = 3

exchange_coeff = (3.0 / 3.141592653589793) ** (1.0 / 3.0)
density_floor = 0.5

F32 = jnp.float32
BF16 = jnp.bfloat16
SMEM = pl.BlockSpec(memory_space=pltpu.SMEM)
VMEM = pl.BlockSpec(memory_space=pltpu.VMEM)
LIMIT = 56 * 1024 * 1024


def swap(value, axis, mask):
    size = lax.axis_size(axis)
    return lax.ppermute(value, axis, [(i, i ^ mask) for i in range(size)])


def tree_sum(values):
    while len(values) > 1:
        values = [values[i] + values[i + 1] for i in range(0, len(values) - 1, 2)] + values[len(values) // 2 * 2 :]
    return values[0]


def row_block(rows):
    for size in (512, 384, 256, 128):
        if rows % size == 0:
            return size
    return rows


def complex_product(g_ref, lower):
    real, imag = lower
    first = jnp.dot(g_ref[0], jnp.concatenate([real, imag], axis=1), preferred_element_type=F32)
    second = jnp.dot(g_ref[1], jnp.concatenate([-imag, real], axis=1), preferred_element_type=F32)
    return first + second


def near_kernel(ids, g_ref, own_ref, partner_ref, acc_ref):
    panels = acc_ref.shape[0]

    @pl.when(pl.program_id(1) == 0)
    def _():
        for q in range(panels):
            acc_ref[q] = complex_product(g_ref, (own_ref[q, 0], own_ref[q, 1]))

    @pl.when(pl.program_id(1) == 1)
    def _():
        for q in range(panels):
            acc_ref[q] += complex_product(g_ref, (partner_ref[q, 0], partner_ref[q, 1]))


def near_product(ids, inverse, own, partner):
    panels, _, rows, width = own.shape
    order = inverse.shape[2]
    tile = row_block(rows)
    whole = pl.BlockSpec(own.shape, lambda m, s, ids: (0, 0, 0, 0), pipeline_mode=pl.Buffered(1))
    return pl.pallas_call(
        near_kernel,
        grid_spec=pltpu.PrefetchScalarGridSpec(
            num_scalar_prefetch=1,
            grid=(rows // tile, 2),
            in_specs=[
                pl.BlockSpec((2, tile, rows), lambda m, s, ids: (0, m, ids[s])),
                whole,
                whole,
            ],
            out_specs=pl.BlockSpec((panels, tile, 2 * width), lambda m, s, ids: (0, m, 0)),
        ),
        out_shape=jax.ShapeDtypeStruct((panels, rows, 2 * width), F32),
        compiler_params=pltpu.CompilerParams(vmem_limit_bytes=LIMIT),
        cost_estimate=pl.CostEstimate(
            flops=2 * 8 * rows * rows * panels * width,
            bytes_accessed=2 * 4 * rows * rows + 4 * panels * rows * 2 * width,
            transcendentals=0,
        ),
        name="near_product",
    )(ids, inverse, own, partner)


def far_kernel(ids, g_ref, left_ref, right_ref, acc_ref, out_ref):
    @pl.when(pl.program_id(1) == 0)
    def _():
        out_ref[...] = acc_ref[...] + complex_product(g_ref, (left_ref[0], left_ref[1]))

    @pl.when(pl.program_id(1) == 1)
    def _():
        out_ref[...] += complex_product(g_ref, (right_ref[0], right_ref[1]))


def last_kernel(
    ids, g_ref, left_ref, right_ref, acc_ref, own_ref, diag_ref, weight_ref, lead_ref, y_in, y_ref, d_ref, sum_ref
):
    m = pl.program_id(0)
    width = y_ref.shape[1]

    @pl.when(pl.program_id(1) == 0)
    def _():
        sum_ref[...] = acc_ref[...] + complex_product(g_ref, (left_ref[0], left_ref[1]))

    @pl.when(pl.program_id(1) == 1)
    def _():
        weight_real = weight_ref[0, 0]
        weight_imag = weight_ref[0, 1]
        total = sum_ref[...] + complex_product(g_ref, (right_ref[0], right_ref[1]))
        real = -total[:, :width]
        imag = -total[:, width:]
        density = weight_real * imag + weight_imag * real
        other = weight_real * real - weight_imag * imag
        y_ref[...] = density.astype(BF16)

        def cross(lower, value):
            high = value.astype(BF16)
            low = (value - high.astype(F32)).astype(BF16)
            both = lax.dot_general(
                lower,
                jnp.concatenate([high, low], axis=1),
                (((0,), (0,)), ((), ())),
                preferred_element_type=F32,
            )
            return both[:, :width] + both[:, width:]

        part = cross(own_ref[0], density) + cross(own_ref[1], other)

        @pl.when(m == 0)
        def _():
            d_ref[...] = lead_ref[0] * (weight_real * diag_ref[1] + weight_imag * diag_ref[0]) - part

        @pl.when(m > 0)
        def _():
            d_ref[...] -= part


def far_product(ids, inverse, left, right, acc, panel):
    _, rows, width = left.shape
    tile = row_block(rows)
    whole = pl.BlockSpec(left.shape, lambda m, s, ids: (0, 0, 0), pipeline_mode=pl.Buffered(1))
    return pl.pallas_call(
        far_kernel,
        grid_spec=pltpu.PrefetchScalarGridSpec(
            num_scalar_prefetch=1,
            grid=(rows // tile, 2),
            in_specs=[
                pl.BlockSpec((2, tile, rows), lambda m, s, ids: (0, m, ids[s])),
                whole,
                whole,
                pl.BlockSpec((None, tile, 2 * width), lambda m, s, ids: (panel, m, 0)),
            ],
            out_specs=pl.BlockSpec((None, tile, 2 * width), lambda m, s, ids: (panel, m, 0)),
        ),
        out_shape=jax.ShapeDtypeStruct(acc.shape, F32),
        input_output_aliases={4: 0},
        compiler_params=pltpu.CompilerParams(vmem_limit_bytes=LIMIT),
        cost_estimate=pl.CostEstimate(
            flops=2 * 8 * rows * rows * width, bytes_accessed=8 * rows * rows, transcendentals=0
        ),
        name="far_product",
    )(ids, inverse, left, right, acc)


def last_product(ids, inverse, left, right, acc, own, diag, weights, lead, density, panel):
    _, rows, width = left.shape
    tile = row_block(rows)
    whole = pl.BlockSpec(left.shape, lambda m, s, ids: (0, 0, 0), pipeline_mode=pl.Buffered(1))
    return pl.pallas_call(
        last_kernel,
        grid_spec=pltpu.PrefetchScalarGridSpec(
            num_scalar_prefetch=1,
            grid=(rows // tile, 2),
            in_specs=[
                pl.BlockSpec((2, tile, rows), lambda m, s, ids: (0, m, ids[s])),
                whole,
                whole,
                pl.BlockSpec((None, tile, 2 * width), lambda m, s, ids: (panel, m, 0)),
                pl.BlockSpec((None, 2, tile, width), lambda m, s, ids: (panel, 0, m, 0)),
                pl.BlockSpec((None, 2, width, width), lambda m, s, ids: (panel, 0, 0, 0)),
                SMEM,
                SMEM,
                pl.BlockSpec(memory_space=pl.ANY),
            ],
            out_specs=[
                pl.BlockSpec((None, tile, width), lambda m, s, ids: (panel, m, 0)),
                pl.BlockSpec((width, width), lambda m, s, ids: (0, 0)),
            ],
            scratch_shapes=[pltpu.VMEM((tile, 2 * width), F32)],
        ),
        out_shape=[
            jax.ShapeDtypeStruct(density.shape, BF16),
            jax.ShapeDtypeStruct((width, width), F32),
        ],
        input_output_aliases={9: 0},
        compiler_params=pltpu.CompilerParams(vmem_limit_bytes=LIMIT),
        cost_estimate=pl.CostEstimate(
            flops=2 * 8 * rows * rows * width, bytes_accessed=8 * rows * rows, transcendentals=0
        ),
        name="last_product",
    )(ids, inverse, left, right, acc, own, diag, weights, lead, density)


def table_kernel(cols, per_device, panels, me_ref, supports, counts, order, send_ref, slot_ref, flags):
    tiles, most = supports.shape
    local_tiles = tiles // cols
    row_blocks = per_device // panels
    me = me_ref[0]

    def clear(i, _):
        flags[i] = 0
        return 0

    lax.fori_loop(0, 2 * cols * per_device, clear, 0)
    offset = cols * per_device

    def mark(t, _):
        dest = t // local_tiles

        def one(k, _):
            block = supports[t, k]
            owner = block // per_device
            local = block - owner * per_device

            @pl.when(owner == me)
            def _():
                flags[dest * per_device + local] = 1

            @pl.when(dest == me)
            def _():
                flags[offset + block] = 1

            return 0

        return lax.fori_loop(0, counts[t], one, 0)

    lax.fori_loop(0, tiles, mark, 0)

    def clear_send(i, _):
        send_ref[i] = 0
        return 0

    lax.fori_loop(0, cols * CAP, clear_send, 0)

    def rank(mask, _):
        other = me ^ mask

        def one(local, found):
            sent, kept = found
            wanted = flags[other * per_device + local]
            row = local // panels

            @pl.when((wanted == 1) & (sent < CAP))
            def _():
                send_ref[mask * CAP + sent] = order[local - row * panels] * row_blocks + row

            place = offset + other * per_device + local
            present = flags[place]
            flags[place] = mask * CAP + jnp.minimum(kept, CAP - 1)
            return sent + wanted, kept + present

        lax.fori_loop(0, per_device, one, (jnp.int32(0), jnp.int32(0)))
        return 0

    lax.fori_loop(0, cols, rank, 0)

    def place(t, _):
        def one(k, _):
            slot_ref[t * most + k] = flags[offset + supports[me * local_tiles + t, k]]
            slot_ref[local_tiles * most + t * most + k] = lax.rem(supports[me * local_tiles + t, k], panels)
            return 0

        lax.fori_loop(0, most, one, 0)
        slot_ref[2 * local_tiles * most + t] = counts[me * local_tiles + t]
        return 0

    lax.fori_loop(0, local_tiles, place, 0)


def tables(me, supports, counts, order, cols, per_device, panels):
    tiles, most = supports.shape
    local_tiles = tiles // cols
    return pl.pallas_call(
        functools.partial(table_kernel, cols, per_device, panels),
        in_specs=[SMEM] * 4,
        out_specs=[SMEM] * 2,
        out_shape=[
            jax.ShapeDtypeStruct((cols * CAP,), jnp.int32),
            jax.ShapeDtypeStruct((local_tiles * (2 * most + 1),), jnp.int32),
        ],
        scratch_shapes=[pltpu.SMEM((2 * cols * per_device,), jnp.int32)],
        name="tables",
    )(me, supports, counts, order)


def pack_kernel(send_ref, y_ref, *rest):
    d_refs, out_refs = rest[: len(rest) - send_ref.shape[0] // CAP], rest[len(rest) - send_ref.shape[0] // CAP :]
    for mask, out_ref in enumerate(out_refs):
        for c in range(CAP):
            out_ref[c] = y_ref[send_ref[mask * CAP + c]]
        for q, d_ref in enumerate(d_refs):
            out_ref[CAP + q] = d_ref[...].astype(BF16)


def pack(send, density, diag_parts, cols):
    width = density.shape[2]
    shape = (CAP + len(diag_parts), width, width)
    return pl.pallas_call(
        pack_kernel,
        in_specs=[SMEM] + [VMEM] * (1 + len(diag_parts)),
        out_specs=[VMEM] * cols,
        out_shape=[jax.ShapeDtypeStruct(shape, BF16)] * cols,
        compiler_params=pltpu.CompilerParams(vmem_limit_bytes=LIMIT),
        name="pack",
    )(send, density.reshape(-1, width, width), *diag_parts)


def join_kernel(*refs):
    parts, out_ref = refs[:-1], refs[-1]
    for mask, part in enumerate(parts):
        for c in range(CAP):
            out_ref[mask * CAP + c] = part[c]
    for q in range(parts[0].shape[0] - CAP):
        total = tree_sum([part[CAP + q].astype(F32) for part in parts])
        out_ref[len(parts) * CAP + q] = total.astype(BF16)


def join(parts):
    width = parts[0].shape[2]
    extra = parts[0].shape[0] - CAP
    return pl.pallas_call(
        join_kernel,
        in_specs=[VMEM] * len(parts),
        out_specs=VMEM,
        out_shape=jax.ShapeDtypeStruct((len(parts) * CAP + extra, width, width), BF16),
        compiler_params=pltpu.CompilerParams(vmem_limit_bytes=LIMIT),
        name="join",
    )(*parts)


def tile_kernel(most, panels, slot_ref, order_ref, row_ref, orbital_ref, core_ref, *rest):
    parts = rest[:-4]
    valence_ref, potential_ref, diag_ref, blocks_ref = rest[-4:]
    t = pl.program_id(0)
    tiles = pl.num_programs(0)
    slots = blocks_ref.shape[0]
    width = blocks_ref.shape[1]

    @pl.when(t == 0)
    def _():
        for s in range(slots):
            total = tree_sum([part[s].astype(F32) for part in parts])
            high = total.astype(BF16)
            blocks_ref[s, :, :width] = high
            blocks_ref[s, :, width:] = (total - high.astype(F32)).astype(BF16)
        for j in range(panels):
            place = slots + order_ref[j]
            diag_ref[j] = tree_sum([part[place].astype(F32) for part in parts])

    count = slot_ref[2 * tiles * most + t]
    valence = jnp.zeros((1, row_ref.shape[-1]), F32)
    for k in range(most):
        values = orbital_ref[slot_ref[tiles * most + t * most + k]]
        mixed = jnp.dot(
            blocks_ref[slot_ref[t * most + k]],
            jnp.concatenate([values, values], axis=0),
            preferred_element_type=F32,
        )
        term = jnp.sum(row_ref[k].astype(F32) * mixed, axis=0, keepdims=True)
        valence = valence + jnp.where(k < count, term, 0.0)
    clamped = jnp.maximum(core_ref[...] + valence, density_floor)
    valence_ref[...] = valence
    potential_ref[...] = -exchange_coeff * clamped ** (1.0 / 3.0)


def tile_stage(slot, order, rows, orbitals, core, parts, cols):
    tiles, most, width, points = rows.shape
    panels = orbitals.shape[1]
    slots = cols * CAP
    flat = pl.BlockSpec((None, 1, points), lambda t: (t, 0, 0))
    valence, potential, diag = pl.pallas_call(
        functools.partial(tile_kernel, most, panels),
        grid=(tiles,),
        in_specs=[
            SMEM,
            SMEM,
            pl.BlockSpec((None, most, width, points), lambda t: (t, 0, 0, 0)),
            pl.BlockSpec((None, panels, width, points), lambda t: (t, 0, 0, 0)),
            flat,
        ]
        + [pl.BlockSpec(parts[0].shape, lambda t: (0, 0, 0), pipeline_mode=pl.Buffered(1))] * len(parts),
        out_specs=[flat, flat, pl.BlockSpec((panels, width, width), lambda t: (0, 0, 0))],
        out_shape=[
            jax.ShapeDtypeStruct((tiles, 1, points), F32),
            jax.ShapeDtypeStruct((tiles, 1, points), F32),
            jax.ShapeDtypeStruct((panels, width, width), F32),
        ],
        scratch_shapes=[pltpu.VMEM((slots, width, 2 * width), BF16)],
        compiler_params=pltpu.CompilerParams(vmem_limit_bytes=LIMIT),
        name="tile_stage",
    )(slot, order, rows, orbitals, core.reshape(tiles, 1, points), *parts)
    return valence.reshape(tiles, points), potential.reshape(tiles, points), diag


def body(
    inverse,
    panels,
    diag_inverse,
    pole_weights,
    supports,
    counts,
    panel_order,
    row_orbitals,
    panel_orbitals,
    core_density,
):
    cols = lax.axis_size("col")
    poles = lax.axis_size("pole")
    me = lax.axis_index("col").astype(jnp.int32)
    matrix = inverse[0]
    own = panels[0]
    diag = diag_inverse[0]
    panel_count, _, rows, width = own.shape
    per_device = rows // width * panel_count
    lead = (me == 0).astype(F32).reshape(1)

    remote = {}
    for step in range(1, cols // 2):
        for q in range(panel_count):
            remote[step, q] = swap(own[q], "col", 2 * step)
    partner = swap(own, "col", 1)
    forward = {key: swap(value, "col", 1) for key, value in remote.items()}

    send, slot = tables(
        me.reshape(1), supports, counts, panel_order, cols, per_device, panel_count
    )
    acc = near_product(jnp.stack([me, me ^ 1]), matrix, own, partner)
    density = jnp.zeros((panel_count, rows, width), BF16)
    diag_parts = []
    for q in range(panel_count):
        for step in range(1, cols // 2):
            ids = jnp.stack([me ^ (2 * step), me ^ (2 * step + 1)])
            left, right = remote[step, q], forward[step, q]
            if step < cols // 2 - 1:
                acc = far_product(ids, matrix, left, right, acc, q)
            else:
                density, diag_part = last_product(
                    ids, matrix, left, right, acc, own, diag, pole_weights, lead, density, q
                )
                diag_parts.append(diag_part)

    messages = pack(send, density, diag_parts, cols)
    arrived = [messages[0]] + [swap(messages[mask], "col", mask) for mask in range(1, cols)]
    joined = join(arrived)
    gathered = [joined] + [swap(joined, "pole", mask) for mask in range(1, poles)]
    return tile_stage(slot, panel_order, row_orbitals, panel_orbitals, core_density, gathered, cols)


def solution(mesh):
    placed = (
        P(("job", "pole"), None, "col", None),
        P(("job", "pole"), None, None, "col", None),
        P(("job", "pole"), None, None, None, None),
        P(("job", "pole"), None),
        P(),
        P(),
        P(),
        P(("job", "col"), None, None, "pole"),
        P(("job", "col"), None, None, "pole"),
        P(("job", "col"), "pole"),
    )
    return jax.shard_map(
        body,
        mesh=mesh,
        in_specs=placed,
        out_specs=(P(("job", "col"), "pole"), P(("job", "col"), "pole"), P("job", None, None)),
        check_vma=False,
    )
```

```python
import functools

import jax
import jax.numpy as jnp
from jax import lax
from jax.experimental import pallas as pl
from jax.experimental.pallas import tpu as pltpu
from jax.sharding import PartitionSpec as P


CAP = 3

exchange_coeff = (3.0 / 3.141592653589793) ** (1.0 / 3.0)
density_floor = 0.5

F32 = jnp.float32
BF16 = jnp.bfloat16
SMEM = pl.BlockSpec(memory_space=pltpu.SMEM)
VMEM = pl.BlockSpec(memory_space=pltpu.VMEM)
LIMIT = 60 * 1024 * 1024


def swap(value, axis, mask):
    size = lax.axis_size(axis)
    return lax.ppermute(value, axis, [(i, i ^ mask) for i in range(size)])


def tree_sum(values):
    while len(values) > 1:
        values = [values[i] + values[i + 1] for i in range(0, len(values) - 1, 2)] + values[len(values) // 2 * 2 :]
    return values[0]


def row_block(rows):
    for size in (512, 384, 256, 128):
        if rows % size == 0:
            return size
    return rows


def complex_product(g_ref, lower):
    real, imag = lower
    first = jnp.dot(g_ref[0], jnp.concatenate([real, imag], axis=1), preferred_element_type=F32)
    second = jnp.dot(g_ref[1], jnp.concatenate([-imag, real], axis=1), preferred_element_type=F32)
    return first + second


def near_kernel(ids, g_ref, own_ref, partner_ref, acc_ref):
    panels = acc_ref.shape[0]

    @pl.when(pl.program_id(1) == 0)
    def _():
        for q in range(panels):
            acc_ref[q] = complex_product(g_ref, (own_ref[q, 0], own_ref[q, 1]))

    @pl.when(pl.program_id(1) == 1)
    def _():
        for q in range(panels):
            acc_ref[q] += complex_product(g_ref, (partner_ref[q, 0], partner_ref[q, 1]))


def near_product(ids, inverse, own, partner):
    panels, _, rows, width = own.shape
    tile = row_block(rows)
    whole = pl.BlockSpec(own.shape, lambda m, s, ids: (0, 0, 0, 0), pipeline_mode=pl.Buffered(1))
    return pl.pallas_call(
        near_kernel,
        grid_spec=pltpu.PrefetchScalarGridSpec(
            num_scalar_prefetch=1,
            grid=(rows // tile, 2),
            in_specs=[
                pl.BlockSpec((2, tile, rows), lambda m, s, ids: (0, m, ids[s])),
                whole,
                whole,
            ],
            out_specs=pl.BlockSpec((panels, tile, 2 * width), lambda m, s, ids: (0, m, 0)),
        ),
        out_shape=jax.ShapeDtypeStruct((panels, rows, 2 * width), F32),
        compiler_params=pltpu.CompilerParams(vmem_limit_bytes=LIMIT),
        cost_estimate=pl.CostEstimate(
            flops=2 * 8 * rows * rows * panels * width,
            bytes_accessed=2 * 4 * rows * rows + 4 * panels * rows * 2 * width,
            transcendentals=0,
        ),
        name="near_product",
    )(ids, inverse, own, partner)


def far_kernel(ids, g_ref, left_ref, right_ref, acc_ref, out_ref):
    @pl.when(pl.program_id(1) == 0)
    def _():
        out_ref[...] = acc_ref[...] + complex_product(g_ref, (left_ref[0], left_ref[1]))

    @pl.when(pl.program_id(1) == 1)
    def _():
        out_ref[...] += complex_product(g_ref, (right_ref[0], right_ref[1]))


def last_kernel(
    poles, ids, g_ref, left_ref, right_ref, acc_ref, own_ref, diag_ref, weight_ref, place_ref, *rest
):
    out_refs, (sum_ref, y_ref, d_ref) = rest[:poles], rest[poles:]
    m = pl.program_id(0)
    steps = pl.num_programs(0)
    tile, width = own_ref.shape[1:]
    count = tile // width
    blocks = y_ref.shape[0]

    @pl.when(pl.program_id(1) == 0)
    def _():
        sum_ref[...] = acc_ref[...] + complex_product(g_ref, (left_ref[0], left_ref[1]))

    @pl.when(pl.program_id(1) == 1)
    def _():
        weight_real = weight_ref[0, 0]
        weight_imag = weight_ref[0, 1]
        total = sum_ref[...] + complex_product(g_ref, (right_ref[0], right_ref[1]))
        real = -total[:, :width]
        imag = -total[:, width:]
        density = weight_real * imag + weight_imag * real
        other = weight_real * real - weight_imag * imag
        y_ref[pl.ds(m * count, count)] = density.reshape(count, poles, width // poles, width)

        def cross(lower, value):
            high = value.astype(BF16)
            low = (value - high.astype(F32)).astype(BF16)
            both = lax.dot_general(
                lower,
                jnp.concatenate([high, low], axis=1),
                (((0,), (0,)), ((), ())),
                preferred_element_type=F32,
            )
            return both[:, :width] + both[:, width:]

        part = (cross(own_ref[0], density) + cross(own_ref[1], other)).reshape(d_ref.shape)

        @pl.when(m == 0)
        def _():
            lead = (place_ref[0] == 0).astype(F32)
            term = lead * (weight_real * diag_ref[1] + weight_imag * diag_ref[0])
            d_ref[...] = term.reshape(d_ref.shape) - part

        @pl.when(m > 0)
        def _():
            d_ref[...] -= part

        @pl.when(m == steps - 1)
        def _():
            for mask, out_ref in enumerate(out_refs):
                other_pole = place_ref[1] ^ mask
                kind = out_ref.dtype
                out_ref[:blocks] = y_ref[:, other_pole].astype(kind)
                diag = d_ref[other_pole]
                high = diag.astype(kind)
                out_ref[blocks] = high
                if kind != F32:
                    out_ref[blocks + 1] = (diag - high.astype(F32)).astype(kind)


def far_product(ids, inverse, left, right, acc, panel):
    _, rows, width = left.shape
    tile = row_block(rows)
    whole = pl.BlockSpec(left.shape, lambda m, s, ids: (0, 0, 0), pipeline_mode=pl.Buffered(1))
    return pl.pallas_call(
        far_kernel,
        grid_spec=pltpu.PrefetchScalarGridSpec(
            num_scalar_prefetch=1,
            grid=(rows // tile, 2),
            in_specs=[
                pl.BlockSpec((2, tile, rows), lambda m, s, ids: (0, m, ids[s])),
                whole,
                whole,
                pl.BlockSpec((None, tile, 2 * width), lambda m, s, ids: (panel, m, 0)),
            ],
            out_specs=pl.BlockSpec((None, tile, 2 * width), lambda m, s, ids: (panel, m, 0)),
        ),
        out_shape=jax.ShapeDtypeStruct(acc.shape, F32),
        input_output_aliases={4: 0},
        compiler_params=pltpu.CompilerParams(vmem_limit_bytes=LIMIT),
        cost_estimate=pl.CostEstimate(
            flops=2 * 8 * rows * rows * width, bytes_accessed=8 * rows * rows, transcendentals=0
        ),
        name="far_product",
    )(ids, inverse, left, right, acc)


def last_product(ids, inverse, left, right, acc, own, diag, weights, place, panel, poles, kind):
    _, rows, width = left.shape
    tile = row_block(rows)
    blocks = rows // width
    depth = width // poles
    whole = pl.BlockSpec(left.shape, lambda m, s, ids: (0, 0, 0), pipeline_mode=pl.Buffered(1))
    shape = (blocks + (1 if kind == F32 else 2), depth, width)
    return pl.pallas_call(
        functools.partial(last_kernel, poles),
        grid_spec=pltpu.PrefetchScalarGridSpec(
            num_scalar_prefetch=1,
            grid=(rows // tile, 2),
            in_specs=[
                pl.BlockSpec((2, tile, rows), lambda m, s, ids: (0, m, ids[s])),
                whole,
                whole,
                pl.BlockSpec((None, tile, 2 * width), lambda m, s, ids: (panel, m, 0)),
                pl.BlockSpec((None, 2, tile, width), lambda m, s, ids: (panel, 0, m, 0)),
                pl.BlockSpec((None, 2, width, width), lambda m, s, ids: (panel, 0, 0, 0)),
                SMEM,
                SMEM,
            ],
            out_specs=[pl.BlockSpec(shape, lambda m, s, ids: (0, 0, 0))] * poles,
            scratch_shapes=[
                pltpu.VMEM((tile, 2 * width), F32),
                pltpu.VMEM((blocks, poles, depth, width), F32),
                pltpu.VMEM((poles, depth, width), F32),
            ],
        ),
        out_shape=[jax.ShapeDtypeStruct(shape, kind)] * poles,
        compiler_params=pltpu.CompilerParams(vmem_limit_bytes=LIMIT),
        cost_estimate=pl.CostEstimate(
            flops=2 * 8 * rows * rows * width, bytes_accessed=8 * rows * rows, transcendentals=0
        ),
        name="last_product",
    )(ids, inverse, left, right, acc, own, diag, weights, place)


def table_kernel(cols, per_device, panels, me_ref, supports, counts, order, send_ref, slot_ref, flags):
    tiles, most = supports.shape
    local_tiles = tiles // cols
    row_blocks = per_device // panels
    me = me_ref[0]

    def clear(i, _):
        flags[i] = 0
        return 0

    lax.fori_loop(0, 2 * cols * per_device, clear, 0)
    offset = cols * per_device

    def mark(t, _):
        dest = t // local_tiles

        def one(k, _):
            block = supports[t, k]
            owner = block // per_device
            local = block - owner * per_device

            @pl.when(owner == me)
            def _():
                flags[dest * per_device + local] = 1

            @pl.when(dest == me)
            def _():
                flags[offset + block] = 1

            return 0

        return lax.fori_loop(0, counts[t], one, 0)

    lax.fori_loop(0, tiles, mark, 0)

    def clear_send(i, _):
        send_ref[i] = 0
        return 0

    lax.fori_loop(0, cols * CAP, clear_send, 0)

    def rank(mask, _):
        other = me ^ mask

        def one(local, found):
            sent, kept = found
            wanted = flags[other * per_device + local]
            row = local // panels

            @pl.when((wanted == 1) & (sent < CAP))
            def _():
                send_ref[mask * CAP + sent] = order[local - row * panels] * row_blocks + row

            place = offset + other * per_device + local
            present = flags[place]
            flags[place] = mask * CAP + jnp.minimum(kept, CAP - 1)
            return sent + wanted, kept + present

        lax.fori_loop(0, per_device, one, (jnp.int32(0), jnp.int32(0)))
        return 0

    lax.fori_loop(0, cols, rank, 0)

    def place(t, _):
        def one(k, _):
            slot_ref[t * most + k] = flags[offset + supports[me * local_tiles + t, k]]
            slot_ref[local_tiles * most + t * most + k] = lax.rem(supports[me * local_tiles + t, k], panels)
            return 0

        lax.fori_loop(0, most, one, 0)
        slot_ref[2 * local_tiles * most + t] = counts[me * local_tiles + t]
        return 0

    lax.fori_loop(0, local_tiles, place, 0)


def tables(me, supports, counts, order, cols, per_device, panels):
    tiles, most = supports.shape
    local_tiles = tiles // cols
    return pl.pallas_call(
        functools.partial(table_kernel, cols, per_device, panels),
        in_specs=[SMEM] * 4,
        out_specs=[SMEM] * 2,
        out_shape=[
            jax.ShapeDtypeStruct((cols * CAP,), jnp.int32),
            jax.ShapeDtypeStruct((local_tiles * (2 * most + 1),), jnp.int32),
        ],
        scratch_shapes=[pltpu.SMEM((2 * cols * per_device,), jnp.int32)],
        name="tables",
    )(me, supports, counts, order)


def total_of(parts, blocks):
    density = tree_sum([part[:blocks].astype(F32) for part in parts])
    diag = [part[blocks].astype(F32) for part in parts]
    if parts[0].dtype != F32:
        diag = [high + part[blocks + 1].astype(F32) for high, part in zip(diag, parts)]
    return density.astype(BF16), tree_sum(diag)


def settle_kernel(poles, blocks, *refs):
    density_ref, diag_ref = refs[-2:]
    for q in range(diag_ref.shape[0]):
        density, diag = total_of(refs[q * poles : (q + 1) * poles], blocks)
        density_ref[q * blocks : (q + 1) * blocks] = density
        diag_ref[q] = diag


def settle(groups, blocks):
    poles = len(groups[0])
    depth, width = groups[0][0].shape[1:]
    return pl.pallas_call(
        functools.partial(settle_kernel, poles, blocks),
        in_specs=[VMEM] * (poles * len(groups)),
        out_specs=[VMEM] * 2,
        out_shape=[
            jax.ShapeDtypeStruct((len(groups) * blocks, depth, width), BF16),
            jax.ShapeDtypeStruct((len(groups), depth, width), F32),
        ],
        compiler_params=pltpu.CompilerParams(vmem_limit_bytes=LIMIT),
        cost_estimate=pl.CostEstimate(flops=1 << 20, bytes_accessed=2 << 20, transcendentals=0),
        name="settle",
    )(*[part for group in groups for part in group])


def pick_kernel(poles, blocks, send_ref, early_ref, early_diag_ref, *rest):
    parts, out_refs, all_ref = rest[:poles], rest[poles:-1], rest[-1]
    early = early_ref.shape[0]
    all_ref[:early] = early_ref[...]
    density, last_diag = total_of(parts, blocks)
    all_ref[early:] = density
    diags = [early_diag_ref[q] for q in range(early_diag_ref.shape[0])] + [last_diag]
    for mask, out_ref in enumerate(out_refs):
        for c in range(CAP):
            out_ref[c] = all_ref[send_ref[mask * CAP + c]]
        for q, diag in enumerate(diags):
            high = diag.astype(BF16)
            out_ref[CAP + 2 * q] = high
            out_ref[CAP + 2 * q + 1] = (diag - high.astype(F32)).astype(BF16)


def pick(send, early, early_diag, parts, blocks, cols):
    poles = len(parts)
    depth, width = early.shape[1:]
    shape = (CAP + 2 * (early_diag.shape[0] + 1), depth, width)
    return pl.pallas_call(
        functools.partial(pick_kernel, poles, blocks),
        in_specs=[SMEM] + [VMEM] * (2 + poles),
        out_specs=[VMEM] * cols,
        out_shape=[jax.ShapeDtypeStruct(shape, BF16)] * cols,
        scratch_shapes=[pltpu.VMEM((early.shape[0] + blocks, depth, width), BF16)],
        compiler_params=pltpu.CompilerParams(vmem_limit_bytes=LIMIT),
        name="pick",
    )(send, early, early_diag, *parts)


def join_kernel(*refs):
    parts, out_ref = refs[:-1], refs[-1]
    for mask, part in enumerate(parts):
        for c in range(CAP):
            out_ref[mask * CAP + c] = part[c]
    for q in range(out_ref.shape[0] - len(parts) * CAP):
        place = CAP + 2 * q
        total = tree_sum([part[place].astype(F32) + part[place + 1].astype(F32) for part in parts])
        out_ref[len(parts) * CAP + q] = total.astype(BF16)


def join(parts):
    depth, width = parts[0].shape[1:]
    extra = (parts[0].shape[0] - CAP) // 2
    return pl.pallas_call(
        join_kernel,
        in_specs=[VMEM] * len(parts),
        out_specs=VMEM,
        out_shape=jax.ShapeDtypeStruct((len(parts) * CAP + extra, depth, width), BF16),
        compiler_params=pltpu.CompilerParams(vmem_limit_bytes=LIMIT),
        name="join",
    )(*parts)


def tile_kernel(most, slot_ref, order_ref, place_ref, row_ref, orbital_ref, core_ref, *rest):
    parts = rest[:-4]
    valence_ref, potential_ref, diag_ref, blocks_ref = rest[-4:]
    t = pl.program_id(0)
    tiles = pl.num_programs(0)
    slots, poles, depth, width = blocks_ref.shape
    panels = diag_ref.shape[0]

    @pl.when(t == 0)
    def _():
        for mask, part in enumerate(parts):
            owner = place_ref[1] ^ mask
            blocks_ref[:, owner] = part[:slots]
            for j in range(panels):
                diag_ref[j, owner] = part[slots + order_ref[j]].astype(F32)

    count = slot_ref[2 * tiles * most + t]
    valence = jnp.zeros((1, row_ref.shape[-1]), F32)
    for k in range(most):
        mixed = jnp.dot(
            blocks_ref[slot_ref[t * most + k]].reshape(poles * depth, width),
            orbital_ref[slot_ref[tiles * most + t * most + k]],
            preferred_element_type=F32,
        )
        term = jnp.sum(row_ref[k].astype(F32) * mixed, axis=0, keepdims=True)
        valence = valence + jnp.where(k < count, term, 0.0)
    clamped = jnp.maximum(core_ref[...] + valence, density_floor)
    valence_ref[...] = valence
    potential_ref[...] = -exchange_coeff * clamped ** (1.0 / 3.0)


def tile_stage(slot, order, place, rows, orbitals, core, parts, cols):
    tiles, most, width, points = rows.shape
    panels = orbitals.shape[1]
    slots = cols * CAP
    poles = len(parts)
    depth = width // poles
    flat = pl.BlockSpec((None, 1, points), lambda t: (t, 0, 0))
    valence, potential, diag = pl.pallas_call(
        functools.partial(tile_kernel, most),
        grid=(tiles,),
        in_specs=[
            SMEM,
            SMEM,
            SMEM,
            pl.BlockSpec((None, most, width, points), lambda t: (t, 0, 0, 0)),
            pl.BlockSpec((None, panels, width, points), lambda t: (t, 0, 0, 0)),
            flat,
        ]
        + [pl.BlockSpec(parts[0].shape, lambda t: (0, 0, 0), pipeline_mode=pl.Buffered(1))] * len(parts),
        out_specs=[flat, flat, pl.BlockSpec((panels, poles, depth, width), lambda t: (0, 0, 0, 0))],
        out_shape=[
            jax.ShapeDtypeStruct((tiles, 1, points), F32),
            jax.ShapeDtypeStruct((tiles, 1, points), F32),
            jax.ShapeDtypeStruct((panels, poles, depth, width), F32),
        ],
        scratch_shapes=[pltpu.VMEM((slots, poles, depth, width), BF16)],
        compiler_params=pltpu.CompilerParams(vmem_limit_bytes=LIMIT),
        name="tile_stage",
    )(slot, order, place, rows, orbitals, core.reshape(tiles, 1, points), *parts)
    return valence.reshape(tiles, points), potential.reshape(tiles, points), diag.reshape(panels, width, width)


def body(
    inverse,
    panels,
    diag_inverse,
    pole_weights,
    supports,
    counts,
    panel_order,
    row_orbitals,
    panel_orbitals,
    core_density,
):
    cols = lax.axis_size("col")
    poles = lax.axis_size("pole")
    me = lax.axis_index("col").astype(jnp.int32)
    my_pole = lax.axis_index("pole").astype(jnp.int32)
    matrix = inverse[0]
    own = panels[0]
    diag = diag_inverse[0]
    panel_count, _, rows, width = own.shape
    blocks = rows // width
    per_device = blocks * panel_count
    place = jnp.stack([me, my_pole])
    steps = range(1, cols // 2)

    partner = swap(own, "col", 1)
    remote = {}
    for step in steps:
        for q in range(panel_count):
            remote[step, q] = swap(own[q], "col", 2 * step)
    forward = {}
    for (step, q), value in remote.items():
        forward[step, q] = swap(value, "col", 1)

    send, slot = tables(me.reshape(1), supports, counts, panel_order, cols, per_device, panel_count)
    acc = near_product(jnp.stack([me, me ^ 1]), matrix, own, partner)
    sums = []
    for q in range(panel_count):
        for step in steps:
            ids = jnp.stack([me ^ (2 * step), me ^ (2 * step + 1)])
            left, right = remote[step, q], forward[step, q]
            if step < cols // 2 - 1:
                acc = far_product(ids, matrix, left, right, acc, q)
            else:
                kind = F32 if q == 0 else BF16
                parts = last_product(
                    ids, matrix, left, right, acc, own, diag, pole_weights, place, q, poles, kind
                )
                group = [parts[0]]
                for mask in range(1, poles):
                    group.append(swap(parts[mask], "pole", mask))
                sums.append(group)

    early, early_diag = settle(sums[:-1], blocks)
    messages = pick(send, early, early_diag, sums[-1], blocks, cols)
    arrived = [messages[0]] + [swap(messages[mask], "col", mask) for mask in range(1, cols)]
    joined = join(arrived)
    gathered = [joined] + [swap(joined, "pole", mask) for mask in range(1, poles)]
    return tile_stage(
        slot, panel_order, place, row_orbitals, panel_orbitals, core_density, gathered, cols
    )


def solution(mesh):
    placed = (
        P(("job", "pole"), None, "col", None),
        P(("job", "pole"), None, None, "col", None),
        P(("job", "pole"), None, None, None, None),
        P(("job", "pole"), None),
        P(),
        P(),
        P(),
        P(("job", "col"), None, None, "pole"),
        P(("job", "col"), None, None, "pole"),
        P(("job", "col"), "pole"),
    )
    return jax.shard_map(
        body,
        mesh=mesh,
        in_specs=placed,
        out_specs=(P(("job", "col"), "pole"), P(("job", "col"), "pole"), P("job", None, None)),
        check_vma=False,
    )
```

```python
import functools

import jax
import jax.numpy as jnp
from jax import lax
from jax.experimental import pallas as pl
from jax.experimental.pallas import tpu as pltpu
from jax.sharding import PartitionSpec as P


CAP = 3

exchange_coeff = (3.0 / 3.141592653589793) ** (1.0 / 3.0)
density_floor = 0.5

F32 = jnp.float32
BF16 = jnp.bfloat16
SMEM = pl.BlockSpec(memory_space=pltpu.SMEM)
VMEM = pl.BlockSpec(memory_space=pltpu.VMEM)
LIMIT = 10 * 1024 * 1024
NEAR_LIMIT = 32 * 1024 * 1024


def swap(value, axis, mask):
    size = lax.axis_size(axis)
    return lax.ppermute(value, axis, [(i, i ^ mask) for i in range(size)])


def tree_sum(values):
    while len(values) > 1:
        values = [values[i] + values[i + 1] for i in range(0, len(values) - 1, 2)] + values[len(values) // 2 * 2 :]
    return values[0]


def row_block(rows):
    for size in (512, 384, 256, 128):
        if rows % size == 0:
            return size
    return rows


def complex_product(g_ref, rows, start, lower):
    real, imag = lower
    columns = pl.ds(start, real.shape[0])
    first = jnp.dot(
        g_ref[0, rows, columns], jnp.concatenate([real, imag], axis=1), preferred_element_type=F32
    )
    second = jnp.dot(
        g_ref[1, rows, columns], jnp.concatenate([-imag, real], axis=1), preferred_element_type=F32
    )
    return first + second


def near_kernel(place_ref, g_hbm, own_ref, partner_ref, acc_ref, far_ref, near_ref, near_sem, far_sem):
    panels, tile, _ = acc_ref.shape
    length, order = g_hbm.shape[1:]
    cols = order // length
    tiles = length // tile
    m = pl.program_id(0)
    me = place_ref[0]
    starts = [pl.multiple_of((me ^ mask) * length, length) for mask in range(cols)]

    def near_copy(step, mask):
        rows = pl.ds(step * tile, tile)
        return pltpu.make_async_copy(
            g_hbm.at[:, rows, pl.ds(starts[mask], length)],
            near_ref.at[:, rows, pl.ds(mask * length, length)],
            near_sem.at[step, mask],
        )

    def far_copy(mask):
        return pltpu.make_async_copy(
            g_hbm.at[:, :, pl.ds(starts[mask], length)],
            far_ref.at[:, :, pl.ds((mask - 2) * length, length)],
            far_sem.at[mask - 2],
        )

    @pl.when(m == 0)
    def _():
        for step in range(tiles):
            for mask in range(2):
                near_copy(step, mask).start()
        for mask in range(2, cols):
            far_copy(mask).start()

    rows = pl.ds(pl.multiple_of(m * tile, tile), tile)
    near_copy(m, 0).wait()
    for q in range(panels):
        acc_ref[q] = complex_product(near_ref, rows, 0, (own_ref[q, 0], own_ref[q, 1]))
    near_copy(m, 1).wait()
    for q in range(panels):
        acc_ref[q] += complex_product(near_ref, rows, length, (partner_ref[q, 0], partner_ref[q, 1]))

    @pl.when(m == tiles - 1)
    def _():
        for mask in range(2, cols):
            far_copy(mask).wait()


def near_product(place, matrix, own, partner):
    panels, _, rows, width = own.shape
    order = matrix.shape[2]
    tile = row_block(rows)
    whole = pl.BlockSpec(own.shape, lambda m: (0, 0, 0, 0), pipeline_mode=pl.Buffered(1))
    return pl.pallas_call(
        near_kernel,
        grid=(rows // tile,),
        in_specs=[SMEM, pl.BlockSpec(memory_space=pl.ANY), whole, whole],
        out_specs=[pl.BlockSpec((panels, tile, 2 * width), lambda m: (0, m, 0)), VMEM],
        out_shape=[
            jax.ShapeDtypeStruct((panels, rows, 2 * width), F32),
            pltpu.VMEM((2, rows, order - 2 * rows), BF16),
        ],
        scratch_shapes=[
            pltpu.VMEM((2, rows, 2 * rows), BF16),
            pltpu.SemaphoreType.DMA((rows // tile, 2)),
            pltpu.SemaphoreType.DMA((order // rows - 2,)),
        ],
        compiler_params=pltpu.CompilerParams(vmem_limit_bytes=NEAR_LIMIT),
        cost_estimate=pl.CostEstimate(
            flops=2 * 8 * rows * rows * panels * width, bytes_accessed=4 * rows * order, transcendentals=0
        ),
        name="near_product",
    )(place, matrix, own, partner)


def far_terms(g_ref, rows, step, offset, left_ref, right_ref):
    length = g_ref.shape[1]
    total = None
    for mask, ref in ((2 * step, left_ref), (2 * step + 1, right_ref)):
        term = complex_product(g_ref, rows, (mask - 2) * length + offset, (ref[0], ref[1]))
        total = term if total is None else total + term
    return total


def far_kernel(step, offset, g_ref, left_ref, right_ref, acc_ref, out_ref):
    tile = out_ref.shape[0]
    rows = pl.ds(pl.multiple_of(pl.program_id(0) * tile, tile), tile)
    out_ref[...] = acc_ref[...] + far_terms(g_ref, rows, step, offset, left_ref, right_ref)


def far_product(g, left, right, acc, panel, step, offset):
    _, depth, width = left.shape
    rows = g.shape[1]
    tile = row_block(rows)
    whole = pl.BlockSpec(left.shape, lambda m: (0, 0, 0), pipeline_mode=pl.Buffered(1))
    return pl.pallas_call(
        functools.partial(far_kernel, step, offset),
        grid=(rows // tile,),
        in_specs=[
            VMEM,
            whole,
            whole,
            pl.BlockSpec((None, tile, 2 * width), lambda m: (panel, m, 0)),
        ],
        out_specs=pl.BlockSpec((None, tile, 2 * width), lambda m: (panel, m, 0)),
        out_shape=jax.ShapeDtypeStruct(acc.shape, F32),
        input_output_aliases={3: 0},
        compiler_params=pltpu.CompilerParams(vmem_limit_bytes=LIMIT),
        cost_estimate=pl.CostEstimate(
            flops=2 * 8 * rows * depth * width, bytes_accessed=8 * rows * width, transcendentals=0
        ),
        name="far_product",
    )(g, left, right, acc)


def last_kernel(
    poles, step, offset, place_ref, g_ref, left_ref, right_ref, acc_ref, own_ref, diag_ref, weight_ref, *rest
):
    out_refs, (y_ref, d_ref) = rest[:poles], rest[poles:]
    m = pl.program_id(0)
    tile, width = own_ref.shape[1:]
    count = tile // width
    blocks = y_ref.shape[0]
    rows = pl.ds(pl.multiple_of(m * tile, tile), tile)

    weight_real = weight_ref[0, 0]
    weight_imag = weight_ref[0, 1]
    total = acc_ref[...] + far_terms(g_ref, rows, step, offset, left_ref, right_ref)
    real = -total[:, :width]
    imag = -total[:, width:]
    density = weight_real * imag + weight_imag * real
    other = weight_real * real - weight_imag * imag
    y_ref[pl.ds(m * count, count)] = density.reshape(count, poles, width // poles, width)

    def cross(lower, value):
        high = value.astype(BF16)
        low = (value - high.astype(F32)).astype(BF16)
        both = lax.dot_general(
            lower,
            jnp.concatenate([high, low], axis=1),
            (((0,), (0,)), ((), ())),
            preferred_element_type=F32,
        )
        return both[:, :width] + both[:, width:]

    part = (cross(own_ref[0], density) + cross(own_ref[1], other)).reshape(d_ref.shape)

    @pl.when(m == 0)
    def _():
        lead = (place_ref[0] == 0).astype(F32)
        term = lead * (weight_real * diag_ref[1] + weight_imag * diag_ref[0])
        d_ref[...] = term.reshape(d_ref.shape) - part

    @pl.when(m > 0)
    def _():
        d_ref[...] -= part

    @pl.when(m == pl.num_programs(0) - 1)
    def _():
        for mask, out_ref in enumerate(out_refs):
            other_pole = place_ref[1] ^ mask
            kind = out_ref.dtype
            out_ref[:blocks] = y_ref[:, other_pole].astype(kind)
            diag = d_ref[other_pole]
            high = diag.astype(kind)
            out_ref[blocks] = high
            if kind != F32:
                out_ref[blocks + 1] = (diag - high.astype(F32)).astype(kind)


def last_product(place, g, left, right, acc, own, diag, weights, panel, step, offset, poles, kind):
    _, depth, width = left.shape
    rows = g.shape[1]
    tile = row_block(rows)
    blocks = rows // width
    whole = pl.BlockSpec(left.shape, lambda m: (0, 0, 0), pipeline_mode=pl.Buffered(1))
    shape = (blocks + (1 if kind == F32 else 2), width // poles, width)
    return pl.pallas_call(
        functools.partial(last_kernel, poles, step, offset),
        grid=(rows // tile,),
        in_specs=[
            SMEM,
            VMEM,
            whole,
            whole,
            pl.BlockSpec((None, tile, 2 * width), lambda m: (panel, m, 0)),
            pl.BlockSpec((None, 2, tile, width), lambda m: (panel, 0, m, 0)),
            pl.BlockSpec((None, 2, width, width), lambda m: (panel, 0, 0, 0)),
            SMEM,
        ],
        out_specs=[pl.BlockSpec(shape, lambda m: (0, 0, 0))] * poles,
        scratch_shapes=[
            pltpu.VMEM((blocks, poles, width // poles, width), F32),
            pltpu.VMEM((poles, width // poles, width), F32),
        ],
        out_shape=[jax.ShapeDtypeStruct(shape, kind)] * poles,
        compiler_params=pltpu.CompilerParams(vmem_limit_bytes=LIMIT),
        cost_estimate=pl.CostEstimate(
            flops=2 * 8 * rows * depth * width, bytes_accessed=8 * rows * width, transcendentals=0
        ),
        name="last_product",
    )(place, g, left, right, acc, own, diag, weights)


def table_kernel(per_device, panels, place_ref, order_ref, supports_ref, counts_ref, send_ref, slot_ref):
    tiles, most = supports_ref.shape
    cols = send_ref.shape[0]
    total = cols * per_device
    me = place_ref[0]
    supports = supports_ref[...]
    counts = counts_ref[...]
    ids = lax.broadcasted_iota(jnp.int32, (tiles, total), 1)
    named = []
    for k in range(most):
        named.append((supports[:, k : k + 1] == ids) & (counts > k))
    any_named = named[0]
    for hit in named[1:]:
        any_named = any_named | hit
    tile_hits = jnp.where(any_named, 1.0, 0.0)
    group_row = lax.broadcasted_iota(jnp.int32, (cols, tiles), 0)
    group_tile = lax.broadcasted_iota(jnp.int32, (cols, tiles), 1)
    group = jnp.where(
        (group_tile >= group_row * (tiles // cols)) & (group_tile < (group_row + 1) * (tiles // cols)), 1.0, 0.0
    )
    needed = jnp.minimum(
        jnp.dot(group.astype(BF16), tile_hits.astype(BF16), preferred_element_type=F32), 1.0
    )
    first = lax.broadcasted_iota(jnp.int32, (total, total), 0)
    second = lax.broadcasted_iota(jnp.int32, (total, total), 1)
    earlier = (first <= second) & (first // per_device == second // per_device)
    rank = jnp.dot(
        needed.astype(BF16), jnp.where(earlier, 1.0, 0.0).astype(BF16), preferred_element_type=F32
    )
    block = lax.broadcasted_iota(jnp.int32, (cols, total), 1)
    dest = lax.broadcasted_iota(jnp.int32, (cols, total), 0)
    owner = block // per_device
    local = block - owner * per_device
    row = local // panels
    spot = local - row * panels
    panel = jnp.zeros_like(spot)
    for j in range(panels):
        panel = jnp.where(spot == j, order_ref[j], panel)
    code = (panel * (per_device // panels) + row).astype(F32)
    mine = (needed > 0.5) & (owner == me)
    lane = lax.broadcasted_iota(jnp.int32, send_ref.shape, 1)
    send = jnp.zeros(send_ref.shape, F32)
    for c in range(CAP):
        value = jnp.sum(jnp.where(mine & (rank == c + 1.0), code, 0.0), axis=1, keepdims=True)
        send = jnp.where(lane == c, value, send)
    send_ref[...] = send.astype(jnp.int32)
    mask = (owner ^ me).astype(F32)
    spots = jnp.where((needed > 0.5) & (dest == me), mask * CAP + jnp.minimum(rank, CAP) - 1.0, 0.0)
    spots = jnp.sum(spots, axis=0, keepdims=True)
    place = lax.broadcasted_iota(jnp.int32, slot_ref.shape, 1)
    slot = jnp.zeros(slot_ref.shape, F32)
    for k, hit in enumerate(named):
        slot = jnp.where(place == k, jnp.sum(jnp.where(hit, spots, 0.0), axis=1, keepdims=True), slot)
    slot_ref[...] = slot.astype(jnp.int32)


def tables(place, supports, counts, order, cols, per_device, panels):
    tiles, most = supports.shape
    return pl.pallas_call(
        functools.partial(table_kernel, per_device, panels),
        in_specs=[SMEM, SMEM, VMEM, VMEM],
        out_specs=[VMEM] * 2,
        out_shape=[
            jax.ShapeDtypeStruct((cols, most), jnp.int32),
            jax.ShapeDtypeStruct((tiles, most), jnp.int32),
        ],
        compiler_params=pltpu.CompilerParams(vmem_limit_bytes=LIMIT),
        cost_estimate=pl.CostEstimate(flops=1 << 20, bytes_accessed=1 << 20, transcendentals=0),
        name="tables",
    )(place, order, supports, counts.reshape(tiles, 1))


def total_of(parts, blocks):
    density = tree_sum([part[:blocks].astype(F32) for part in parts])
    diag = [part[blocks].astype(F32) for part in parts]
    if parts[0].dtype != F32:
        diag = [high + part[blocks + 1].astype(F32) for high, part in zip(diag, parts)]
    return density.astype(BF16), tree_sum(diag)


def settle_kernel(poles, blocks, *refs):
    density_ref, diag_ref = refs[-2:]
    for q in range(diag_ref.shape[0]):
        density, diag = total_of(refs[q * poles : (q + 1) * poles], blocks)
        density_ref[q * blocks : (q + 1) * blocks] = density
        diag_ref[q] = diag


def settle(groups, blocks):
    poles = len(groups[0])
    depth, width = groups[0][0].shape[1:]
    return pl.pallas_call(
        functools.partial(settle_kernel, poles, blocks),
        in_specs=[VMEM] * (poles * len(groups)),
        out_specs=[VMEM] * 2,
        out_shape=[
            jax.ShapeDtypeStruct((len(groups) * blocks, depth, width), BF16),
            jax.ShapeDtypeStruct((len(groups), depth, width), F32),
        ],
        compiler_params=pltpu.CompilerParams(vmem_limit_bytes=LIMIT),
        cost_estimate=pl.CostEstimate(flops=1 << 20, bytes_accessed=2 << 20, transcendentals=0),
        name="settle",
    )(*[part for group in groups for part in group])


def pick_kernel(poles, blocks, place_ref, send_ref, early_ref, early_diag_ref, *rest):
    parts, out_refs, all_ref = rest[:poles], rest[poles:-1], rest[-1]
    early = early_ref.shape[0]
    all_ref[:early] = early_ref[...]
    density, last_diag = total_of(parts, blocks)
    all_ref[early:] = density
    diags = [early_diag_ref[q] for q in range(early_diag_ref.shape[0])] + [last_diag]
    for mask, out_ref in enumerate(out_refs):
        for c in range(CAP):
            out_ref[c] = all_ref[send_ref[place_ref[0] ^ mask, c]]
        for q, diag in enumerate(diags):
            high = diag.astype(BF16)
            out_ref[CAP + 2 * q] = high
            out_ref[CAP + 2 * q + 1] = (diag - high.astype(F32)).astype(BF16)


def pick(place, send, early, early_diag, parts, blocks, cols):
    poles = len(parts)
    depth, width = early.shape[1:]
    shape = (CAP + 2 * (early_diag.shape[0] + 1), depth, width)
    return pl.pallas_call(
        functools.partial(pick_kernel, poles, blocks),
        in_specs=[SMEM, SMEM] + [VMEM] * (2 + poles),
        out_specs=[VMEM] * cols,
        out_shape=[jax.ShapeDtypeStruct(shape, BF16)] * cols,
        scratch_shapes=[pltpu.VMEM((early.shape[0] + blocks, depth, width), BF16)],
        compiler_params=pltpu.CompilerParams(vmem_limit_bytes=LIMIT),
        name="pick",
    )(place, send, early, early_diag, *parts)


def join_kernel(*refs):
    parts, out_ref = refs[:-1], refs[-1]
    for mask, part in enumerate(parts):
        for c in range(CAP):
            out_ref[mask * CAP + c] = part[c]
    for q in range(out_ref.shape[0] - len(parts) * CAP):
        place = CAP + 2 * q
        total = tree_sum([part[place].astype(F32) + part[place + 1].astype(F32) for part in parts])
        out_ref[len(parts) * CAP + q] = total.astype(BF16)


def join(parts):
    depth, width = parts[0].shape[1:]
    extra = (parts[0].shape[0] - CAP) // 2
    return pl.pallas_call(
        join_kernel,
        in_specs=[VMEM] * len(parts),
        out_specs=VMEM,
        out_shape=jax.ShapeDtypeStruct((len(parts) * CAP + extra, depth, width), BF16),
        compiler_params=pltpu.CompilerParams(vmem_limit_bytes=LIMIT),
        name="join",
    )(*parts)


def tile_kernel(
    place_ref, order_ref, slot_ref, supports_ref, counts_ref, row_ref, orbital_ref, core_ref, *rest
):
    parts = rest[:-4]
    valence_ref, potential_ref, diag_ref, blocks_ref = rest[-4:]
    tiles, most = row_ref.shape[:2]
    slots, poles, depth, width = blocks_ref.shape
    panels = diag_ref.shape[0]
    first = place_ref[0] * tiles

    for mask, part in enumerate(parts):
        owner = place_ref[1] ^ mask
        blocks_ref[:, owner] = part[:slots]
        for j in range(panels):
            diag_ref[j, owner] = part[slots + order_ref[j]].astype(F32)

    def one(t, _):
        valence = jnp.zeros((1, row_ref.shape[-1]), F32)
        for k in range(most):
            mixed = jnp.dot(
                blocks_ref[slot_ref[first + t, k]].reshape(poles * depth, width),
                orbital_ref[t, lax.rem(supports_ref[first + t, k], panels)],
                preferred_element_type=F32,
            )
            term = jnp.sum(row_ref[t, k].astype(F32) * mixed, axis=0, keepdims=True)
            valence = valence + jnp.where(k < counts_ref[first + t], term, 0.0)
        valence_ref[t] = valence
        return 0

    lax.fori_loop(0, tiles, one, 0, unroll=True)
    clamped = jnp.maximum(core_ref[...] + valence_ref[...], density_floor)
    potential_ref[...] = -exchange_coeff * clamped ** (1.0 / 3.0)


def tile_stage(place, order, slot, supports, counts, rows, orbitals, core, parts, cols):
    tiles, _, width, points = rows.shape
    panels = orbitals.shape[1]
    slots = cols * CAP
    poles = len(parts)
    depth = width // poles
    valence, potential, diag = pl.pallas_call(
        tile_kernel,
        in_specs=[SMEM] * 5 + [VMEM] * (3 + poles),
        out_specs=[VMEM] * 3,
        out_shape=[
            jax.ShapeDtypeStruct((tiles, 1, points), F32),
            jax.ShapeDtypeStruct((tiles, 1, points), F32),
            jax.ShapeDtypeStruct((panels, poles, depth, width), F32),
        ],
        scratch_shapes=[pltpu.VMEM((slots, poles, depth, width), BF16)],
        compiler_params=pltpu.CompilerParams(vmem_limit_bytes=LIMIT),
        name="tile_stage",
    )(place, order, slot, supports, counts, rows, orbitals, core.reshape(tiles, 1, points), *parts)
    return valence.reshape(tiles, points), potential.reshape(tiles, points), diag.reshape(panels, width, width)


def body(
    inverse,
    panels,
    diag_inverse,
    pole_weights,
    supports,
    counts,
    panel_order,
    row_orbitals,
    panel_orbitals,
    core_density,
):
    cols = lax.axis_size("col")
    poles = lax.axis_size("pole")
    me = lax.axis_index("col").astype(jnp.int32)
    my_pole = lax.axis_index("pole").astype(jnp.int32)
    matrix = inverse[0]
    own = panels[0]
    diag = diag_inverse[0]
    panel_count, _, rows, width = own.shape
    blocks = rows // width
    per_device = blocks * panel_count
    place = jnp.stack([me, my_pole])
    steps = range(1, cols // 2)

    pieces = []
    for q in range(panel_count):
        parts = 2 if q == panel_count - 1 else 1
        pieces += [(q, part * (rows // parts), rows // parts) for part in range(parts)]

    remote = {}
    source = own
    for piece, (q, offset, depth) in enumerate(pieces):
        part = source[q, :, offset : offset + depth]
        if piece == 0:
            part, source = lax.optimization_barrier((part, own))
        for step in steps:
            remote[step, piece] = swap(part, "col", 2 * step)
    partner = swap(own, "col", 1)
    forward = {}
    for (step, piece), value in remote.items():
        forward[step, piece] = swap(value, "col", 1)

    send, slot = tables(place, supports, counts, panel_order, cols, per_device, panel_count)
    acc, staged = near_product(place, matrix, own, partner)
    sums = []
    for piece, (q, offset, depth) in enumerate(pieces):
        for step in steps:
            left, right = remote[step, piece], forward[step, piece]
            if step < cols // 2 - 1 or offset + depth < rows:
                acc = far_product(staged, left, right, acc, q, step, offset)
                continue
            kind = F32 if q == 0 else BF16
            parts = last_product(place, staged, left, right, acc, own, diag, pole_weights, q, step, offset, poles, kind)
            group = [parts[0]]
            for mask in range(1, poles):
                group.append(swap(parts[mask], "pole", mask))
            sums.append(group)

    early, early_diag = settle(sums[:-1], blocks)
    messages = pick(place, send, early, early_diag, sums[-1], blocks, cols)
    arrived = [messages[0]] + [swap(messages[mask], "col", mask) for mask in range(1, cols)]
    joined = join(arrived)
    gathered = [joined] + [swap(joined, "pole", mask) for mask in range(1, poles)]
    return tile_stage(
        place,
        panel_order,
        slot,
        supports,
        counts,
        row_orbitals,
        panel_orbitals,
        core_density,
        gathered,
        cols,
    )


def solution(mesh):
    placed = (
        P(("job", "pole"), None, "col", None),
        P(("job", "pole"), None, None, "col", None),
        P(("job", "pole"), None, None, None, None),
        P(("job", "pole"), None),
        P(),
        P(),
        P(),
        P(("job", "col"), None, None, "pole"),
        P(("job", "col"), None, None, "pole"),
        P(("job", "col"), "pole"),
    )
    return jax.shard_map(
        body,
        mesh=mesh,
        in_specs=placed,
        out_specs=(P(("job", "col"), "pole"), P(("job", "col"), "pole"), P("job", None, None)),
        check_vma=False,
    )
```

```python
import functools

import jax
import jax.numpy as jnp
from jax import lax
from jax.experimental import pallas as pl
from jax.experimental.pallas import tpu as pltpu
from jax.sharding import PartitionSpec as P


CAP = 3

exchange_coeff = (3.0 / 3.141592653589793) ** (1.0 / 3.0)
density_floor = 0.5

F32 = jnp.float32
BF16 = jnp.bfloat16
SMEM = pl.BlockSpec(memory_space=pltpu.SMEM)
VMEM = pl.BlockSpec(memory_space=pltpu.VMEM)
LIMIT = 10 * 1024 * 1024
NEAR_LIMIT = 26 * 1024 * 1024


def swap(value, axis, mask):
    size = lax.axis_size(axis)
    return lax.ppermute(value, axis, [(i, i ^ mask) for i in range(size)])


def tree_sum(values):
    while len(values) > 1:
        values = [values[i] + values[i + 1] for i in range(0, len(values) - 1, 2)] + values[len(values) // 2 * 2 :]
    return values[0]


def row_block(rows):
    for size in (512, 384, 256, 128):
        if rows % size == 0:
            return size
    return rows


def near_block(rows):
    return 384 if rows % 384 == 0 else row_block(rows)


def complex_product(g_ref, rows, start, lower):
    real, imag = lower
    columns = pl.ds(start, real.shape[0])
    first = jnp.dot(
        g_ref[0, rows, columns], jnp.concatenate([real, imag], axis=1), preferred_element_type=F32
    )
    second = jnp.dot(
        g_ref[1, rows, columns], jnp.concatenate([-imag, real], axis=1), preferred_element_type=F32
    )
    return first + second


def near_kernel(g_hbm, own_ref, partner_ref, *rest):
    acc_refs, (far_ref, near_ref, near_sem, far_sem) = rest[:-4], rest[-4:]
    length, order = g_hbm.shape[1:]
    cols = order // length
    tile = near_block(length)
    tiles = length // tile
    m = pl.program_id(0)
    me = lax.axis_index("col")
    starts = [pl.multiple_of((me ^ mask) * length, length) for mask in range(cols)]

    def near_copy(step, mask):
        rows = pl.ds(step * tile, tile)
        return pltpu.make_async_copy(
            g_hbm.at[:, rows, pl.ds(starts[mask], length)],
            near_ref.at[:, rows, pl.ds(mask * length, length)],
            near_sem.at[step, mask],
        )

    def far_copy(mask):
        return pltpu.make_async_copy(
            g_hbm.at[:, :, pl.ds(starts[mask], length)],
            far_ref.at[:, :, pl.ds((mask - 2) * length, length)],
            far_sem.at[mask - 2],
        )

    @pl.when(m == 0)
    def _():
        near_copy(0, 0).start()
        near_copy(0, 1).start()

    near_copy(m, 0).wait()

    @pl.when(m == 0)
    def _():
        for step in range(1, tiles):
            near_copy(step, 0).start()
            near_copy(step, 1).start()

    @pl.when(m == min(1, tiles - 1))
    def _():
        for mask in range(2, cols):
            far_copy(mask).start()

    near_copy(m, 1).wait()
    rows = pl.ds(pl.multiple_of(m * tile, tile), tile)
    for q, acc_ref in enumerate(acc_refs):
        acc_ref[rows] = complex_product(
            near_ref, rows, 0, (own_ref[q, 0], own_ref[q, 1])
        ) + complex_product(near_ref, rows, length, (partner_ref[q, 0], partner_ref[q, 1]))

    @pl.when(m == tiles - 1)
    def _():
        for mask in range(2, cols):
            far_copy(mask).wait()


def near_product(matrix, own, partner):
    panels, _, rows, width = own.shape
    order = matrix.shape[2]
    tile = near_block(rows)
    results = pl.pallas_call(
        near_kernel,
        grid=(rows // tile,),
        in_specs=[pl.BlockSpec(memory_space=pl.ANY), VMEM, VMEM],
        out_specs=[VMEM] * (panels + 1),
        out_shape=[pltpu.VMEM((rows, 2 * width), F32)] * panels
        + [pltpu.VMEM((2, rows, order - 2 * rows), BF16)],
        scratch_shapes=[
            pltpu.VMEM((2, rows, 2 * rows), BF16),
            pltpu.SemaphoreType.DMA((rows // tile, 2)),
            pltpu.SemaphoreType.DMA((order // rows - 2,)),
        ],
        compiler_params=pltpu.CompilerParams(vmem_limit_bytes=NEAR_LIMIT),
        cost_estimate=pl.CostEstimate(
            flops=2 * 8 * rows * rows * panels * width, bytes_accessed=4 * rows * order, transcendentals=0
        ),
        name="near_product",
    )(matrix, own, partner)
    return list(results[:-1]), results[-1]


def far_terms(g_ref, rows, step, offset, left_ref, right_ref):
    length = g_ref.shape[1]
    total = None
    for mask, ref in ((2 * step, left_ref), (2 * step + 1, right_ref)):
        term = complex_product(g_ref, rows, (mask - 2) * length + offset, (ref[0], ref[1]))
        total = term if total is None else total + term
    return total


def far_kernel(step, offset, g_ref, left_ref, right_ref, acc_ref, out_ref):
    tile = row_block(out_ref.shape[0])
    rows = pl.ds(pl.multiple_of(pl.program_id(0) * tile, tile), tile)
    out_ref[rows] = acc_ref[rows] + far_terms(g_ref, rows, step, offset, left_ref, right_ref)


def far_product(g, left, right, acc, step, offset):
    _, depth, width = left.shape
    rows = g.shape[1]
    tile = row_block(rows)
    whole = pl.BlockSpec(left.shape, lambda m: (0, 0, 0), pipeline_mode=pl.Buffered(1))
    return pl.pallas_call(
        functools.partial(far_kernel, step, offset),
        grid=(rows // tile,),
        in_specs=[
            VMEM,
            whole,
            whole,
            VMEM,
        ],
        out_specs=VMEM,
        out_shape=pltpu.VMEM(acc.shape, F32),
        compiler_params=pltpu.CompilerParams(vmem_limit_bytes=LIMIT),
        cost_estimate=pl.CostEstimate(
            flops=2 * 8 * rows * depth * width, bytes_accessed=8 * rows * width, transcendentals=0
        ),
        name="far_product",
    )(g, left, right, acc)


def last_kernel(
    poles, step, offset, g_ref, left_ref, right_ref, acc_ref, own_ref, diag_ref, weight_ref, *rest
):
    out_refs, (y_ref, d_ref) = rest[:poles], rest[poles:]
    m = pl.program_id(0)
    tile, width = own_ref.shape[1:]
    count = tile // width
    blocks = y_ref.shape[0]
    rows = pl.ds(pl.multiple_of(m * tile, tile), tile)

    weight_real = weight_ref[0, 0]
    weight_imag = weight_ref[0, 1]
    total = acc_ref[rows] + far_terms(g_ref, rows, step, offset, left_ref, right_ref)
    real = -total[:, :width]
    imag = -total[:, width:]
    density = weight_real * imag + weight_imag * real
    other = weight_real * real - weight_imag * imag
    y_ref[pl.ds(m * count, count)] = density.reshape(count, poles, width // poles, width)

    def cross(lower, value):
        high = value.astype(BF16)
        low = (value - high.astype(F32)).astype(BF16)
        both = lax.dot_general(
            lower,
            jnp.concatenate([high, low], axis=1),
            (((0,), (0,)), ((), ())),
            preferred_element_type=F32,
        )
        return both[:, :width] + both[:, width:]

    part = (cross(own_ref[0], density) + cross(own_ref[1], other)).reshape(d_ref.shape)

    @pl.when(m == 0)
    def _():
        lead = (lax.axis_index("col") == 0).astype(F32)
        term = lead * (weight_real * diag_ref[1] + weight_imag * diag_ref[0])
        d_ref[...] = term.reshape(d_ref.shape) - part

    @pl.when(m > 0)
    def _():
        d_ref[...] -= part

    @pl.when(m == pl.num_programs(0) - 1)
    def _():
        for mask, out_ref in enumerate(out_refs):
            other_pole = lax.axis_index("pole") ^ mask
            kind = out_ref.dtype
            out_ref[:blocks] = y_ref[:, other_pole].astype(kind)
            diag = d_ref[other_pole]
            high = diag.astype(kind)
            out_ref[blocks] = high
            if kind != F32:
                out_ref[blocks + 1] = (diag - high.astype(F32)).astype(kind)


def last_product(g, left, right, acc, own, diag, weights, panel, step, offset, poles, kind):
    _, depth, width = left.shape
    rows = g.shape[1]
    tile = row_block(rows)
    blocks = rows // width
    whole = pl.BlockSpec(left.shape, lambda m: (0, 0, 0), pipeline_mode=pl.Buffered(1))
    shape = (blocks + (1 if kind == F32 else 2), width // poles, width)
    return pl.pallas_call(
        functools.partial(last_kernel, poles, step, offset),
        grid=(rows // tile,),
        in_specs=[
            VMEM,
            whole,
            whole,
            VMEM,
            pl.BlockSpec((None, 2, tile, width), lambda m: (panel, 0, m, 0)),
            pl.BlockSpec((None, 2, width, width), lambda m: (panel, 0, 0, 0)),
            SMEM,
        ],
        out_specs=[pl.BlockSpec(shape, lambda m: (0, 0, 0))] * poles,
        scratch_shapes=[
            pltpu.VMEM((blocks, poles, width // poles, width), F32),
            pltpu.VMEM((poles, width // poles, width), F32),
        ],
        out_shape=[jax.ShapeDtypeStruct(shape, kind)] * poles,
        compiler_params=pltpu.CompilerParams(vmem_limit_bytes=LIMIT),
        cost_estimate=pl.CostEstimate(
            flops=2 * 8 * rows * depth * width, bytes_accessed=8 * rows * width, transcendentals=0
        ),
        name="last_product",
    )(g, left, right, acc, own, diag, weights)


def table_kernel(per_device, panels, cols, order_ref, supports_ref, counts_ref, send_ref, plan_ref):
    most, tiles = supports_ref.shape
    total = cols * per_device
    me = lax.axis_index("col")
    supports = supports_ref[...]
    counts = counts_ref[...]
    ids = lax.broadcasted_iota(jnp.int32, (total, tiles), 0)
    named = [(supports[k : k + 1] == ids) & (counts > k) for k in range(most)]
    any_named = named[0]
    for hit in named[1:]:
        any_named = any_named | hit
    tile_hits = jnp.where(any_named, 1.0, 0.0).astype(BF16)
    share = tiles // cols
    group_tile = lax.broadcasted_iota(jnp.int32, (tiles, cols), 0)
    group_col = lax.broadcasted_iota(jnp.int32, (tiles, cols), 1)
    group = (group_tile >= group_col * share) & (group_tile < (group_col + 1) * share)
    needed = jnp.minimum(
        jnp.dot(tile_hits, jnp.where(group, 1.0, 0.0).astype(BF16), preferred_element_type=F32), 1.0
    )
    first = lax.broadcasted_iota(jnp.int32, (total, total), 0)
    second = lax.broadcasted_iota(jnp.int32, (total, total), 1)
    earlier = (second <= first) & (first // per_device == second // per_device)
    rank = jnp.dot(
        jnp.where(earlier, 1.0, 0.0).astype(BF16), needed.astype(BF16), preferred_element_type=F32
    )
    block = lax.broadcasted_iota(jnp.int32, (total, cols), 0)
    dest = lax.broadcasted_iota(jnp.int32, (total, cols), 1)
    owner = block // per_device
    local = block - owner * per_device
    row = local // panels
    spot = local - row * panels
    panel = jnp.zeros_like(spot)
    for j in range(panels):
        panel = jnp.where(spot == j, order_ref[j], panel)
    code = (panel * (per_device // panels) + row).astype(F32)
    mine = (needed > 0.5) & (owner == me)
    for c in range(CAP):
        value = jnp.sum(jnp.where(mine & (rank == c + 1.0), code, 0.0), axis=0, keepdims=True)
        send_ref[c : c + 1] = value.astype(jnp.int32)
    lane = lax.broadcasted_iota(jnp.int32, (1, cols), 1)
    order = jnp.zeros((1, cols), jnp.int32)
    for j in range(panels):
        order = jnp.where(lane == j, order_ref[j], order)
    send_ref[CAP : CAP + 1] = order
    mask = (owner ^ me).astype(F32)
    spots = jnp.where((needed > 0.5) & (dest == me), mask * CAP + jnp.minimum(rank, CAP) - 1.0, 0.0)
    spots = jnp.sum(spots, axis=1, keepdims=True)
    for k, hit in enumerate(named):
        slot = jnp.sum(jnp.where(hit, spots, 0.0), axis=0, keepdims=True)
        plan_ref[k : k + 1] = slot.astype(jnp.int32)
    plan_ref[most : 2 * most] = lax.rem(supports, panels)
    plan_ref[2 * most : 2 * most + 1] = counts


def tables(supports, counts, order, cols, per_device, panels):
    tiles, most = supports.shape
    return pl.pallas_call(
        functools.partial(table_kernel, per_device, panels, cols),
        in_specs=[SMEM, VMEM, VMEM],
        out_specs=[VMEM] * 2,
        out_shape=[
            jax.ShapeDtypeStruct((CAP + 1, cols), jnp.int32),
            jax.ShapeDtypeStruct((2 * most + 1, tiles), jnp.int32),
        ],
        compiler_params=pltpu.CompilerParams(vmem_limit_bytes=LIMIT),
        cost_estimate=pl.CostEstimate(flops=1 << 20, bytes_accessed=1 << 20, transcendentals=0),
        name="tables",
    )(order, supports.T, counts.reshape(1, tiles))


def total_of(parts, blocks):
    density = tree_sum([part[:blocks].astype(F32) for part in parts])
    diag = [part[blocks].astype(F32) for part in parts]
    if parts[0].dtype != F32:
        diag = [high + part[blocks + 1].astype(F32) for high, part in zip(diag, parts)]
    return density.astype(BF16), tree_sum(diag)


def settle_kernel(poles, blocks, *refs):
    density_ref, diag_ref = refs[-2:]
    for q in range(diag_ref.shape[0]):
        density, diag = total_of(refs[q * poles : (q + 1) * poles], blocks)
        density_ref[q * blocks : (q + 1) * blocks] = density
        diag_ref[q] = diag


def settle(groups, blocks):
    poles = len(groups[0])
    depth, width = groups[0][0].shape[1:]
    return pl.pallas_call(
        functools.partial(settle_kernel, poles, blocks),
        in_specs=[VMEM] * (poles * len(groups)),
        out_specs=[VMEM] * 2,
        out_shape=[
            jax.ShapeDtypeStruct((len(groups) * blocks, depth, width), BF16),
            jax.ShapeDtypeStruct((len(groups), depth, width), F32),
        ],
        compiler_params=pltpu.CompilerParams(vmem_limit_bytes=LIMIT),
        cost_estimate=pl.CostEstimate(flops=1 << 20, bytes_accessed=2 << 20, transcendentals=0),
        name="settle",
    )(*[part for group in groups for part in group])


def pick_kernel(poles, blocks, send_ref, early_ref, early_diag_ref, *rest):
    parts, out_refs, (all_ref, diag_ref) = rest[:poles], rest[poles:-2], rest[-2:]
    early = early_ref.shape[0]
    panels = diag_ref.shape[0]
    me = lax.axis_index("col")
    all_ref[:early] = early_ref[...]
    density, last_diag = total_of(parts, blocks)
    all_ref[early:] = density
    diag_ref[: panels - 1] = early_diag_ref[...]
    diag_ref[panels - 1] = last_diag
    for mask, out_ref in enumerate(out_refs):
        for c in range(CAP):
            out_ref[c] = all_ref[send_ref[c, me ^ mask]]
    for j in range(panels):
        diag = diag_ref[send_ref[CAP, j]]
        high = diag.astype(BF16)
        low = (diag - high.astype(F32)).astype(BF16)
        for out_ref in out_refs:
            out_ref[CAP + 2 * j] = high
            out_ref[CAP + 2 * j + 1] = low


def pick(send, early, early_diag, parts, blocks, cols):
    poles = len(parts)
    depth, width = early.shape[1:]
    panels = early_diag.shape[0] + 1
    shape = (CAP + 2 * panels, depth, width)
    return pl.pallas_call(
        functools.partial(pick_kernel, poles, blocks),
        in_specs=[SMEM] + [VMEM] * (2 + poles),
        out_specs=[VMEM] * cols,
        out_shape=[jax.ShapeDtypeStruct(shape, BF16)] * cols,
        scratch_shapes=[
            pltpu.VMEM((early.shape[0] + blocks, depth, width), BF16),
            pltpu.VMEM((panels, depth, width), F32),
        ],
        compiler_params=pltpu.CompilerParams(vmem_limit_bytes=LIMIT),
        name="pick",
    )(send, early, early_diag, *parts)


def join_kernel(*refs):
    parts, out_ref = refs[:-1], refs[-1]
    for mask, part in enumerate(parts):
        for c in range(CAP):
            out_ref[mask * CAP + c] = part[c]
    for q in range(out_ref.shape[0] - len(parts) * CAP):
        place = CAP + 2 * q
        total = tree_sum([part[place].astype(F32) + part[place + 1].astype(F32) for part in parts])
        out_ref[len(parts) * CAP + q] = total.astype(BF16)


def join(parts):
    depth, width = parts[0].shape[1:]
    extra = (parts[0].shape[0] - CAP) // 2
    return pl.pallas_call(
        join_kernel,
        in_specs=[VMEM] * len(parts),
        out_specs=VMEM,
        out_shape=jax.ShapeDtypeStruct((len(parts) * CAP + extra, depth, width), BF16),
        compiler_params=pltpu.CompilerParams(vmem_limit_bytes=LIMIT),
        name="join",
    )(*parts)


def tile_kernel(plan_ref, row_ref, orbital_ref, core_hbm, *rest):
    parts = rest[:-6]
    valence_ref, potential_ref, diag_ref, blocks_ref, core_ref, core_sem = rest[-6:]
    tiles, most = row_ref.shape[:2]
    slots, poles, depth, width = blocks_ref.shape
    panels = diag_ref.shape[0]
    first = lax.axis_index("col") * tiles
    core_copy = pltpu.make_async_copy(core_hbm, core_ref, core_sem)
    core_copy.start()

    for mask, part in enumerate(parts):
        owner = lax.axis_index("pole") ^ mask
        blocks_ref[:, owner] = part[:slots]
        for j in range(panels):
            diag_ref[j, owner] = part[slots + j].astype(F32)

    def one(t, _):
        valence = jnp.zeros((1, row_ref.shape[-1]), F32)
        for k in range(most):
            mixed = jnp.dot(
                blocks_ref[plan_ref[k, first + t]].reshape(poles * depth, width),
                orbital_ref[t, plan_ref[most + k, first + t]],
                preferred_element_type=F32,
            )
            term = jnp.sum(row_ref[t, k].astype(F32) * mixed, axis=0, keepdims=True)
            valence = valence + jnp.where(k < plan_ref[2 * most, first + t], term, 0.0)
        valence_ref[pl.ds(t, 1)] = valence
        return 0

    lax.fori_loop(0, tiles, one, 0, unroll=True)
    core_copy.wait()
    clamped = jnp.maximum(core_ref[...] + valence_ref[...], density_floor)
    potential_ref[...] = -exchange_coeff * clamped ** (1.0 / 3.0)


def tile_stage(plan, rows, orbitals, core, parts, cols):
    _, _, width, _ = rows.shape
    panels = orbitals.shape[1]
    slots = cols * CAP
    poles = len(parts)
    depth = width // poles
    valence, potential, diag = pl.pallas_call(
        tile_kernel,
        in_specs=[SMEM, VMEM, VMEM, pl.BlockSpec(memory_space=pl.ANY)] + [VMEM] * poles,
        out_specs=[VMEM] * 3,
        out_shape=[
            jax.ShapeDtypeStruct(core.shape, F32),
            jax.ShapeDtypeStruct(core.shape, F32),
            jax.ShapeDtypeStruct((panels, poles, depth, width), F32),
        ],
        scratch_shapes=[
            pltpu.VMEM((slots, poles, depth, width), BF16),
            pltpu.VMEM(core.shape, F32),
            pltpu.SemaphoreType.DMA(()),
        ],
        compiler_params=pltpu.CompilerParams(vmem_limit_bytes=LIMIT),
        name="tile_stage",
    )(plan, rows, orbitals, core, *parts)
    return valence, potential, diag.reshape(panels, width, width)


def body(
    inverse,
    panels,
    diag_inverse,
    pole_weights,
    supports,
    counts,
    panel_order,
    row_orbitals,
    panel_orbitals,
    core_density,
):
    cols = lax.axis_size("col")
    poles = lax.axis_size("pole")
    matrix = inverse[0]
    own = panels[0]
    diag = diag_inverse[0]
    panel_count, _, rows, width = own.shape
    blocks = rows // width
    per_device = blocks * panel_count
    steps = range(1, cols // 2)

    pieces = []
    for q in range(panel_count):
        parts = 2 if q == panel_count - 1 else 1
        pieces += [(q, part * (rows // parts), rows // parts) for part in range(parts)]

    partner = swap(own, "col", 1)
    remote = {}
    for piece, (q, offset, depth) in enumerate(pieces):
        for step in steps:
            remote[step, piece] = swap(own[q, :, offset : offset + depth], "col", 2 * step)
    forward = {}
    for (step, piece), value in remote.items():
        forward[step, piece] = swap(value, "col", 1)

    send, plan = tables(supports, counts, panel_order, cols, per_device, panel_count)
    acc, staged = near_product(matrix, own, partner)
    sums = []
    for piece, (q, offset, depth) in enumerate(pieces):
        for step in steps:
            left, right = remote[step, piece], forward[step, piece]
            if step < cols // 2 - 1 or offset + depth < rows:
                acc[q] = far_product(staged, left, right, acc[q], step, offset)
                continue
            kind = F32 if q == 0 else BF16
            parts = last_product(
                staged, left, right, acc[q], own, diag, pole_weights, q, step, offset, poles, kind
            )
            group = [parts[0]]
            for mask in range(1, poles):
                group.append(swap(parts[mask], "pole", mask))
            sums.append(group)

    early, early_diag = settle(sums[:-1], blocks)
    messages = pick(send, early, early_diag, sums[-1], blocks, cols)
    arrived = [messages[0]] + [swap(messages[mask], "col", mask) for mask in range(1, cols)]
    joined = join(arrived)
    gathered = [joined]
    for mask in range(1, poles):
        gathered.append(swap(joined, "pole", mask))
    return tile_stage(plan, row_orbitals, panel_orbitals, core_density, gathered, cols)


def solution(mesh):
    placed = (
        P(("job", "pole"), None, "col", None),
        P(("job", "pole"), None, None, "col", None),
        P(("job", "pole"), None, None, None, None),
        P(("job", "pole"), None),
        P(),
        P(),
        P(),
        P(("job", "col"), None, None, "pole"),
        P(("job", "col"), None, None, "pole"),
        P(("job", "col"), "pole"),
    )
    return jax.shard_map(
        body,
        mesh=mesh,
        in_specs=placed,
        out_specs=(P(("job", "col"), "pole"), P(("job", "col"), "pole"), P("job", None, None)),
        check_vma=False,
    )
```

```python
import functools

import jax
import jax.numpy as jnp
from jax import lax
from jax.experimental import pallas as pl
from jax.experimental.pallas import tpu as pltpu
from jax.sharding import PartitionSpec as P


CAP = 3

exchange_coeff = (3.0 / 3.141592653589793) ** (1.0 / 3.0)
density_floor = 0.5

F32 = jnp.float32
BF16 = jnp.bfloat16
SMEM = pl.BlockSpec(memory_space=pltpu.SMEM)
VMEM = pl.BlockSpec(memory_space=pltpu.VMEM)
LIMIT = 10 * 1024 * 1024
NEAR_LIMIT = 26 * 1024 * 1024


def swap(value, axis, mask):
    size = lax.axis_size(axis)
    return lax.ppermute(value, axis, [(i, i ^ mask) for i in range(size)])


def tree_sum(values):
    while len(values) > 1:
        values = [values[i] + values[i + 1] for i in range(0, len(values) - 1, 2)] + values[len(values) // 2 * 2 :]
    return values[0]


def row_block(rows):
    for size in (512, 384, 256, 128):
        if rows % size == 0:
            return size
    return rows


def near_block(rows):
    return 384 if rows % 384 == 0 else row_block(rows)


def complex_product(g_ref, rows, start, lower):
    real, imag = lower
    columns = pl.ds(start, real.shape[0])
    first = jnp.dot(
        g_ref[0, rows, columns], jnp.concatenate([real, imag], axis=1), preferred_element_type=F32
    )
    second = jnp.dot(
        g_ref[1, rows, columns], jnp.concatenate([-imag, real], axis=1), preferred_element_type=F32
    )
    return first + second


def near_kernel(g_hbm, own_ref, partner_ref, *rest):
    acc_refs, (far_ref, near_ref, near_sem, far_sem) = rest[:-4], rest[-4:]
    length, order = g_hbm.shape[1:]
    cols = order // length
    tile = near_block(length)
    tiles = length // tile
    m = pl.program_id(0)
    me = lax.axis_index("col")
    starts = [pl.multiple_of((me ^ mask) * length, length) for mask in range(cols)]

    def near_copy(step, mask):
        rows = pl.ds(step * tile, tile)
        return pltpu.make_async_copy(
            g_hbm.at[:, rows, pl.ds(starts[mask], length)],
            near_ref.at[:, rows, pl.ds(mask * length, length)],
            near_sem.at[step, mask],
        )

    def far_copy(mask):
        return pltpu.make_async_copy(
            g_hbm.at[:, :, pl.ds(starts[mask], length)],
            far_ref.at[:, :, pl.ds((mask - 2) * length, length)],
            far_sem.at[mask - 2],
        )

    @pl.when(m == 0)
    def _():
        near_copy(0, 0).start()
        near_copy(0, 1).start()

    near_copy(m, 0).wait()

    @pl.when(m == 0)
    def _():
        for step in range(1, tiles):
            near_copy(step, 0).start()
            near_copy(step, 1).start()

    @pl.when(m == min(1, tiles - 1))
    def _():
        for mask in range(2, cols):
            far_copy(mask).start()

    near_copy(m, 1).wait()
    rows = pl.ds(pl.multiple_of(m * tile, tile), tile)
    for q, acc_ref in enumerate(acc_refs):
        acc_ref[rows] = complex_product(
            near_ref, rows, 0, (own_ref[q, 0], own_ref[q, 1])
        ) + complex_product(near_ref, rows, length, (partner_ref[q, 0], partner_ref[q, 1]))

    @pl.when(m == tiles - 1)
    def _():
        for mask in range(2, cols):
            far_copy(mask).wait()


def near_product(matrix, own, partner):
    panels, _, rows, width = own.shape
    order = matrix.shape[2]
    tile = near_block(rows)
    results = pl.pallas_call(
        near_kernel,
        grid=(rows // tile,),
        in_specs=[pl.BlockSpec(memory_space=pl.ANY), VMEM, VMEM],
        out_specs=[VMEM] * (panels + 1),
        out_shape=[pltpu.VMEM((rows, 2 * width), F32)] * panels
        + [pltpu.VMEM((2, rows, order - 2 * rows), BF16)],
        scratch_shapes=[
            pltpu.VMEM((2, rows, 2 * rows), BF16),
            pltpu.SemaphoreType.DMA((rows // tile, 2)),
            pltpu.SemaphoreType.DMA((order // rows - 2,)),
        ],
        compiler_params=pltpu.CompilerParams(vmem_limit_bytes=NEAR_LIMIT),
        cost_estimate=pl.CostEstimate(
            flops=2 * 8 * rows * rows * panels * width, bytes_accessed=4 * rows * order, transcendentals=0
        ),
        name="near_product",
    )(matrix, own, partner)
    return list(results[:-1]), results[-1]


def far_terms(g_ref, rows, step, offset, left_ref, right_ref):
    length = g_ref.shape[1]
    total = None
    for mask, ref in ((2 * step, left_ref), (2 * step + 1, right_ref)):
        term = complex_product(g_ref, rows, (mask - 2) * length + offset, (ref[0], ref[1]))
        total = term if total is None else total + term
    return total


def far_kernel(step, offset, g_ref, left_ref, right_ref, acc_ref, out_ref):
    tile = row_block(out_ref.shape[0])
    rows = pl.ds(pl.multiple_of(pl.program_id(0) * tile, tile), tile)
    out_ref[rows] = acc_ref[rows] + far_terms(g_ref, rows, step, offset, left_ref, right_ref)


def far_product(g, left, right, acc, step, offset):
    _, depth, width = left.shape
    rows = g.shape[1]
    tile = row_block(rows)
    whole = pl.BlockSpec(left.shape, lambda m: (0, 0, 0), pipeline_mode=pl.Buffered(1))
    return pl.pallas_call(
        functools.partial(far_kernel, step, offset),
        grid=(rows // tile,),
        in_specs=[
            VMEM,
            whole,
            whole,
            VMEM,
        ],
        out_specs=VMEM,
        out_shape=pltpu.VMEM(acc.shape, F32),
        compiler_params=pltpu.CompilerParams(vmem_limit_bytes=LIMIT),
        cost_estimate=pl.CostEstimate(
            flops=2 * 8 * rows * depth * width, bytes_accessed=8 * rows * width, transcendentals=0
        ),
        name="far_product",
    )(g, left, right, acc)


def last_kernel(
    poles, step, offset, g_ref, left_ref, right_ref, acc_ref, own_ref, diag_ref, weight_ref, *rest
):
    out_refs, (y_ref, d_ref) = rest[:poles], rest[poles:]
    m = pl.program_id(0)
    tile, width = own_ref.shape[1:]
    count = tile // width
    blocks = y_ref.shape[0]
    rows = pl.ds(pl.multiple_of(m * tile, tile), tile)

    weight_real = weight_ref[0, 0]
    weight_imag = weight_ref[0, 1]
    total = acc_ref[rows] + far_terms(g_ref, rows, step, offset, left_ref, right_ref)
    real = -total[:, :width]
    imag = -total[:, width:]
    density = weight_real * imag + weight_imag * real
    other = weight_real * real - weight_imag * imag
    y_ref[pl.ds(m * count, count)] = density.reshape(count, poles, width // poles, width)

    def cross(lower, value):
        high = value.astype(BF16)
        low = (value - high.astype(F32)).astype(BF16)
        both = lax.dot_general(
            lower,
            jnp.concatenate([high, low], axis=1),
            (((0,), (0,)), ((), ())),
            preferred_element_type=F32,
        )
        return both[:, :width] + both[:, width:]

    part = (cross(own_ref[0], density) + cross(own_ref[1], other)).reshape(d_ref.shape)

    @pl.when(m == 0)
    def _():
        lead = (lax.axis_index("col") == 0).astype(F32)
        term = lead * (weight_real * diag_ref[1] + weight_imag * diag_ref[0])
        d_ref[...] = term.reshape(d_ref.shape) - part

    @pl.when(m > 0)
    def _():
        d_ref[...] -= part

    @pl.when(m == pl.num_programs(0) - 1)
    def _():
        for mask, out_ref in enumerate(out_refs):
            other_pole = lax.axis_index("pole") ^ mask
            kind = out_ref.dtype
            out_ref[:blocks] = y_ref[:, other_pole].astype(kind)
            out_ref[blocks] = d_ref[other_pole].astype(kind)


def last_product(g, left, right, acc, own, diag, weights, panel, step, offset, poles, kind):
    _, depth, width = left.shape
    rows = g.shape[1]
    tile = row_block(rows)
    blocks = rows // width
    whole = pl.BlockSpec(left.shape, lambda m: (0, 0, 0), pipeline_mode=pl.Buffered(1))
    shape = (blocks + 1, width // poles, width)
    return pl.pallas_call(
        functools.partial(last_kernel, poles, step, offset),
        grid=(rows // tile,),
        in_specs=[
            VMEM,
            whole,
            whole,
            VMEM,
            pl.BlockSpec((None, 2, tile, width), lambda m: (panel, 0, m, 0)),
            pl.BlockSpec((None, 2, width, width), lambda m: (panel, 0, 0, 0)),
            SMEM,
        ],
        out_specs=[pl.BlockSpec(shape, lambda m: (0, 0, 0))] * poles,
        scratch_shapes=[
            pltpu.VMEM((blocks, poles, width // poles, width), F32),
            pltpu.VMEM((poles, width // poles, width), F32),
        ],
        out_shape=[jax.ShapeDtypeStruct(shape, kind)] * poles,
        compiler_params=pltpu.CompilerParams(vmem_limit_bytes=LIMIT),
        cost_estimate=pl.CostEstimate(
            flops=2 * 8 * rows * depth * width, bytes_accessed=8 * rows * width, transcendentals=0
        ),
        name="last_product",
    )(g, left, right, acc, own, diag, weights)


def table_kernel(per_device, panels, cols, order_ref, supports_ref, counts_ref, send_ref, plan_ref):
    most, tiles = supports_ref.shape
    total = cols * per_device
    me = lax.axis_index("col")
    supports = supports_ref[...]
    counts = counts_ref[...]
    ids = lax.broadcasted_iota(jnp.int32, (total, tiles), 0)
    named = [(supports[k : k + 1] == ids) & (counts > k) for k in range(most)]
    any_named = named[0]
    for hit in named[1:]:
        any_named = any_named | hit
    tile_hits = jnp.where(any_named, 1.0, 0.0).astype(BF16)
    share = tiles // cols
    group_tile = lax.broadcasted_iota(jnp.int32, (tiles, cols), 0)
    group_col = lax.broadcasted_iota(jnp.int32, (tiles, cols), 1)
    group = (group_tile >= group_col * share) & (group_tile < (group_col + 1) * share)
    needed = jnp.minimum(
        jnp.dot(tile_hits, jnp.where(group, 1.0, 0.0).astype(BF16), preferred_element_type=F32), 1.0
    )
    first = lax.broadcasted_iota(jnp.int32, (total, total), 0)
    second = lax.broadcasted_iota(jnp.int32, (total, total), 1)
    earlier = (second <= first) & (first // per_device == second // per_device)
    rank = jnp.dot(
        jnp.where(earlier, 1.0, 0.0).astype(BF16), needed.astype(BF16), preferred_element_type=F32
    )
    block = lax.broadcasted_iota(jnp.int32, (total, cols), 0)
    dest = lax.broadcasted_iota(jnp.int32, (total, cols), 1)
    owner = block // per_device
    local = block - owner * per_device
    row = local // panels
    spot = local - row * panels
    panel = jnp.zeros_like(spot)
    for j in range(panels):
        panel = jnp.where(spot == j, order_ref[j], panel)
    code = (panel * (per_device // panels) + row).astype(F32)
    mine = (needed > 0.5) & (owner == me)
    for c in range(CAP):
        value = jnp.sum(jnp.where(mine & (rank == c + 1.0), code, 0.0), axis=0, keepdims=True)
        send_ref[c : c + 1] = value.astype(jnp.int32)
    lane = lax.broadcasted_iota(jnp.int32, (1, tiles), 1)
    order = jnp.zeros((1, tiles), jnp.int32)
    for j in range(panels):
        order = jnp.where(lane == j, order_ref[j], order)
    plan_ref[2 * most + 1 : 2 * most + 2] = order
    mask = (owner ^ me).astype(F32)
    spots = jnp.where((needed > 0.5) & (dest == me), mask * CAP + jnp.minimum(rank, CAP) - 1.0, 0.0)
    spots = jnp.sum(spots, axis=1, keepdims=True)
    for k, hit in enumerate(named):
        slot = jnp.sum(jnp.where(hit, spots, 0.0), axis=0, keepdims=True)
        plan_ref[k : k + 1] = slot.astype(jnp.int32)
    plan_ref[most : 2 * most] = lax.rem(supports, panels)
    plan_ref[2 * most : 2 * most + 1] = counts


def tables(supports, counts, order, cols, per_device, panels):
    tiles, most = supports.shape
    return pl.pallas_call(
        functools.partial(table_kernel, per_device, panels, cols),
        in_specs=[SMEM, VMEM, VMEM],
        out_specs=[VMEM] * 2,
        out_shape=[
            jax.ShapeDtypeStruct((CAP, cols), jnp.int32),
            jax.ShapeDtypeStruct((2 * most + 2, tiles), jnp.int32),
        ],
        compiler_params=pltpu.CompilerParams(vmem_limit_bytes=LIMIT),
        cost_estimate=pl.CostEstimate(flops=1 << 20, bytes_accessed=1 << 20, transcendentals=0),
        name="tables",
    )(order, supports.T, counts.reshape(1, tiles))


def total_of(parts, blocks):
    density = tree_sum([part[:blocks].astype(F32) for part in parts])
    return density.astype(BF16), tree_sum([part[blocks].astype(F32) for part in parts])


def settle_kernel(poles, blocks, *refs):
    density_ref, diag_ref = refs[-2:]
    for q in range(diag_ref.shape[0]):
        density, diag = total_of(refs[q * poles : (q + 1) * poles], blocks)
        density_ref[q * blocks : (q + 1) * blocks] = density
        diag_ref[q] = diag


def settle(groups, blocks):
    poles = len(groups[0])
    depth, width = groups[0][0].shape[1:]
    return pl.pallas_call(
        functools.partial(settle_kernel, poles, blocks),
        in_specs=[VMEM] * (poles * len(groups)),
        out_specs=[VMEM] * 2,
        out_shape=[
            jax.ShapeDtypeStruct((len(groups) * blocks, depth, width), BF16),
            jax.ShapeDtypeStruct((len(groups), depth, width), F32),
        ],
        compiler_params=pltpu.CompilerParams(vmem_limit_bytes=LIMIT),
        cost_estimate=pl.CostEstimate(flops=1 << 20, bytes_accessed=2 << 20, transcendentals=0),
        name="settle",
    )(*[part for group in groups for part in group])


def pick_kernel(poles, blocks, send_ref, early_ref, *rest):
    parts, out_refs, all_ref = rest[:poles], rest[poles:-1], rest[-1]
    early = early_ref.shape[0]
    me = lax.axis_index("col")
    all_ref[:early] = early_ref[...]
    density, diag = total_of(parts, blocks)
    all_ref[early:] = density
    for mask, out_ref in enumerate(out_refs):
        for c in range(CAP):
            out_ref[c] = all_ref[send_ref[c, me ^ mask]]
        out_ref[CAP] = diag.astype(BF16)


def pick(send, early, parts, blocks, cols):
    poles = len(parts)
    depth, width = early.shape[1:]
    return pl.pallas_call(
        functools.partial(pick_kernel, poles, blocks),
        in_specs=[SMEM] + [VMEM] * (1 + poles),
        out_specs=[VMEM] * cols,
        out_shape=[jax.ShapeDtypeStruct((CAP + 1, depth, width), BF16)] * cols,
        scratch_shapes=[pltpu.VMEM((early.shape[0] + blocks, depth, width), BF16)],
        compiler_params=pltpu.CompilerParams(vmem_limit_bytes=LIMIT),
        name="pick",
    )(send, early, *parts)


def near_join_kernel(diag_ref, *refs):
    parts, out_ref = refs[:-1], refs[-1]
    end = len(parts) * CAP
    for place, part in enumerate(parts):
        out_ref[place * CAP : (place + 1) * CAP] = part[:CAP]
    out_ref[end:] = diag_ref[...].astype(BF16)


def far_join_kernel(skip, *refs):
    parts, out_ref = refs[:-1], refs[-1]
    for place, part in enumerate(parts[skip:]):
        out_ref[place * CAP : (place + 1) * CAP] = part[:CAP]
    out_ref[out_ref.shape[0] - 1] = tree_sum([part[CAP].astype(F32) for part in parts]).astype(BF16)


def join(kernel, operands, slots):
    depth, width = operands[0].shape[1:]
    return pl.pallas_call(
        kernel,
        in_specs=[VMEM] * len(operands),
        out_specs=VMEM,
        out_shape=jax.ShapeDtypeStruct((slots, depth, width), BF16),
        compiler_params=pltpu.CompilerParams(vmem_limit_bytes=LIMIT),
    )(*operands)


def add_kernel(*refs):
    refs[-1][...] = tree_sum([ref[...] for ref in refs[:-1]])


def add(parts):
    return pl.pallas_call(
        add_kernel,
        in_specs=[VMEM] * len(parts),
        out_specs=VMEM,
        out_shape=jax.ShapeDtypeStruct(parts[0].shape, F32),
        compiler_params=pltpu.CompilerParams(vmem_limit_bytes=LIMIT),
        name="add",
    )(*parts)


def tile_kernel(plan_ref, row_ref, orbital_ref, core_hbm, *rest):
    poles = (len(rest) - 7) // 2
    near_parts, far_parts = rest[:poles], rest[poles : 2 * poles]
    valence_ref, potential_ref, diag_ref, blocks_ref, raw_ref, core_ref, core_sem = rest[-7:]
    tiles, most = row_ref.shape[:2]
    slots, poles, depth, width = blocks_ref.shape
    panels = diag_ref.shape[0]
    first = lax.axis_index("col") * tiles
    core_copy = pltpu.make_async_copy(core_hbm, core_ref, core_sem)
    core_copy.start()

    first_slots = 2 * CAP
    for mask, (near, far) in enumerate(zip(near_parts, far_parts)):
        owner = lax.axis_index("pole") ^ mask
        blocks_ref[:first_slots, owner] = near[:first_slots]
        blocks_ref[first_slots:, owner] = far[: slots - first_slots]
        raw_ref[: panels - 1, owner] = near[first_slots:]
        raw_ref[panels - 1, owner] = far[slots - first_slots]
    for j in range(panels):
        diag_ref[j] = raw_ref[plan_ref[2 * most + 1, j]].astype(F32)

    def one(t, _):
        valence = jnp.zeros((1, row_ref.shape[-1]), F32)
        for k in range(most):
            mixed = jnp.dot(
                blocks_ref[plan_ref[k, first + t]].reshape(poles * depth, width),
                orbital_ref[t, plan_ref[most + k, first + t]],
                preferred_element_type=F32,
            )
            term = jnp.sum(row_ref[t, k].astype(F32) * mixed, axis=0, keepdims=True)
            valence = valence + jnp.where(k < plan_ref[2 * most, first + t], term, 0.0)
        valence_ref[pl.ds(t, 1)] = valence
        return 0

    lax.fori_loop(0, tiles, one, 0, unroll=True)
    core_copy.wait()
    clamped = jnp.maximum(core_ref[...] + valence_ref[...], density_floor)
    potential_ref[...] = -exchange_coeff * clamped ** (1.0 / 3.0)


def tile_stage(plan, rows, orbitals, core, near_parts, far_parts, cols):
    _, _, width, _ = rows.shape
    panels = orbitals.shape[1]
    slots = cols * CAP
    poles = len(near_parts)
    depth = width // poles
    valence, potential, diag = pl.pallas_call(
        tile_kernel,
        in_specs=[SMEM, VMEM, VMEM, pl.BlockSpec(memory_space=pl.ANY)] + [VMEM] * (2 * poles),
        out_specs=[VMEM] * 3,
        out_shape=[
            jax.ShapeDtypeStruct(core.shape, F32),
            jax.ShapeDtypeStruct(core.shape, F32),
            jax.ShapeDtypeStruct((panels, poles, depth, width), F32),
        ],
        scratch_shapes=[
            pltpu.VMEM((slots, poles, depth, width), BF16),
            pltpu.VMEM((panels, poles, depth, width), BF16),
            pltpu.VMEM(core.shape, F32),
            pltpu.SemaphoreType.DMA(()),
        ],
        compiler_params=pltpu.CompilerParams(vmem_limit_bytes=LIMIT),
        name="tile_stage",
    )(plan, rows, orbitals, core, *near_parts, *far_parts)
    return valence, potential, diag.reshape(panels, width, width)


def body(
    inverse,
    panels,
    diag_inverse,
    pole_weights,
    supports,
    counts,
    panel_order,
    row_orbitals,
    panel_orbitals,
    core_density,
):
    cols = lax.axis_size("col")
    poles = lax.axis_size("pole")
    matrix = inverse[0]
    own = panels[0]
    diag = diag_inverse[0]
    panel_count, _, rows, width = own.shape
    blocks = rows // width
    per_device = blocks * panel_count
    steps = range(1, cols // 2)

    pieces = []
    for q in range(panel_count):
        parts = 2 if q == panel_count - 1 else 1
        pieces += [(q, part * (rows // parts), rows // parts) for part in range(parts)]

    partner = swap(own, "col", 1)
    remote = {}
    for piece, (q, offset, depth) in enumerate(pieces):
        for step in steps:
            remote[step, piece] = swap(own[q, :, offset : offset + depth], "col", 2 * step)
    forward = {}
    for (step, piece), value in remote.items():
        forward[step, piece] = swap(value, "col", 1)

    send, plan = tables(supports, counts, panel_order, cols, per_device, panel_count)
    acc, staged = near_product(matrix, own, partner)
    sums = []
    for piece, (q, offset, depth) in enumerate(pieces):
        for step in steps:
            left, right = remote[step, piece], forward[step, piece]
            if step < cols // 2 - 1 or offset + depth < rows:
                acc[q] = far_product(staged, left, right, acc[q], step, offset)
                continue
            kind = F32 if q == 0 else BF16
            parts = last_product(
                staged, left, right, acc[q], own, diag, pole_weights, q, step, offset, poles, kind
            )
            group = [parts[0]]
            for mask in range(1, poles):
                group.append(swap(parts[mask], "pole", mask))
            sums.append(group)

    early, early_diag = settle(sums[:-1], blocks)
    spread = [early_diag]
    for mask in range(1, cols):
        spread.append(swap(early_diag, "col", mask))
    diag_rows = add(spread)
    messages = pick(send, early, sums[-1], blocks, cols)
    arrived = [messages[0]]
    for mask in range(1, cols):
        arrived.append(swap(messages[mask], "col", mask))
    panels_early = diag_rows.shape[0]
    near = join(near_join_kernel, [diag_rows] + arrived[:2], 2 * CAP + panels_early)
    gathered_near = [near]
    for mask in range(1, poles):
        gathered_near.append(swap(near, "pole", mask))
    far = join(functools.partial(far_join_kernel, 2), arrived, (cols - 2) * CAP + 1)
    gathered_far = [far]
    for mask in range(1, poles):
        gathered_far.append(swap(far, "pole", mask))
    return tile_stage(plan, row_orbitals, panel_orbitals, core_density, gathered_near, gathered_far, cols)


def solution(mesh):
    placed = (
        P(("job", "pole"), None, "col", None),
        P(("job", "pole"), None, None, "col", None),
        P(("job", "pole"), None, None, None, None),
        P(("job", "pole"), None),
        P(),
        P(),
        P(),
        P(("job", "col"), None, None, "pole"),
        P(("job", "col"), None, None, "pole"),
        P(("job", "col"), "pole"),
    )
    return jax.shard_map(
        body,
        mesh=mesh,
        in_specs=placed,
        out_specs=(P(("job", "col"), "pole"), P(("job", "col"), "pole"), P("job", None, None)),
        check_vma=False,
    )
```

```python
import functools

import jax
import jax.numpy as jnp
from jax import lax
from jax.experimental import pallas as pl
from jax.experimental.pallas import tpu as pltpu
from jax.sharding import PartitionSpec as P


CAP = 3

exchange_coeff = (3.0 / 3.141592653589793) ** (1.0 / 3.0)
density_floor = 0.5

F32 = jnp.float32
BF16 = jnp.bfloat16
SMEM = pl.BlockSpec(memory_space=pltpu.SMEM)
VMEM = pl.BlockSpec(memory_space=pltpu.VMEM)
LIMIT = 10 * 1024 * 1024
NEAR_LIMIT = 26 * 1024 * 1024


def swap(value, axis, mask):
    size = lax.axis_size(axis)
    return lax.ppermute(value, axis, [(i, i ^ mask) for i in range(size)])


def tree_sum(values):
    while len(values) > 1:
        values = [values[i] + values[i + 1] for i in range(0, len(values) - 1, 2)] + values[len(values) // 2 * 2 :]
    return values[0]


def row_block(rows):
    for size in (512, 384, 256, 128):
        if rows % size == 0:
            return size
    return rows


def near_block(rows):
    return 384 if rows % 384 == 0 else row_block(rows)


def complex_product(g_ref, rows, start, lower):
    real, imag = lower
    columns = pl.ds(start, real.shape[0])
    first = jnp.dot(
        g_ref[0, rows, columns], jnp.concatenate([real, imag], axis=1), preferred_element_type=F32
    )
    second = jnp.dot(
        g_ref[1, rows, columns], jnp.concatenate([-imag, real], axis=1), preferred_element_type=F32
    )
    return first + second


def near_kernel(g_hbm, own_ref, partner_ref, *rest):
    acc_refs, (far_ref, near_ref, near_sem, far_sem) = rest[:-4], rest[-4:]
    length, order = g_hbm.shape[1:]
    cols = order // length
    tile = near_block(length)
    tiles = length // tile
    m = pl.program_id(0)
    me = lax.axis_index("col")
    starts = [pl.multiple_of((me ^ mask) * length, length) for mask in range(cols)]

    def near_copy(step, mask):
        rows = pl.ds(step * tile, tile)
        return pltpu.make_async_copy(
            g_hbm.at[:, rows, pl.ds(starts[mask], length)],
            near_ref.at[:, rows, pl.ds(mask * length, length)],
            near_sem.at[step, mask],
        )

    def far_copy(mask):
        return pltpu.make_async_copy(
            g_hbm.at[:, :, pl.ds(starts[mask], length)],
            far_ref.at[:, :, pl.ds((mask - 2) * length, length)],
            far_sem.at[mask - 2],
        )

    @pl.when(m == 0)
    def _():
        near_copy(0, 0).start()
        near_copy(0, 1).start()

    near_copy(m, 0).wait()

    @pl.when(m == 0)
    def _():
        for step in range(1, tiles):
            near_copy(step, 0).start()
            near_copy(step, 1).start()

    @pl.when(m == min(1, tiles - 1))
    def _():
        for mask in range(2, cols):
            far_copy(mask).start()

    near_copy(m, 1).wait()
    rows = pl.ds(pl.multiple_of(m * tile, tile), tile)
    for q, acc_ref in enumerate(acc_refs):
        acc_ref[rows] = complex_product(
            near_ref, rows, 0, (own_ref[q, 0], own_ref[q, 1])
        ) + complex_product(near_ref, rows, length, (partner_ref[q, 0], partner_ref[q, 1]))

    @pl.when(m == tiles - 1)
    def _():
        for mask in range(2, cols):
            far_copy(mask).wait()


def near_product(matrix, own, partner):
    panels, _, rows, width = own.shape
    order = matrix.shape[2]
    tile = near_block(rows)
    results = pl.pallas_call(
        near_kernel,
        grid=(rows // tile,),
        in_specs=[pl.BlockSpec(memory_space=pl.ANY), VMEM, VMEM],
        out_specs=[VMEM] * (panels + 1),
        out_shape=[pltpu.VMEM((rows, 2 * width), F32)] * panels
        + [pltpu.VMEM((2, rows, order - 2 * rows), BF16)],
        scratch_shapes=[
            pltpu.VMEM((2, rows, 2 * rows), BF16),
            pltpu.SemaphoreType.DMA((rows // tile, 2)),
            pltpu.SemaphoreType.DMA((order // rows - 2,)),
        ],
        compiler_params=pltpu.CompilerParams(vmem_limit_bytes=NEAR_LIMIT),
        cost_estimate=pl.CostEstimate(
            flops=2 * 8 * rows * rows * panels * width, bytes_accessed=4 * rows * order, transcendentals=0
        ),
        name="near_product",
    )(matrix, own, partner)
    return list(results[:-1]), results[-1]


def far_terms(g_ref, rows, step, offset, left_ref, right_ref):
    length = g_ref.shape[1]
    total = None
    for mask, ref in ((2 * step, left_ref), (2 * step + 1, right_ref)):
        term = complex_product(g_ref, rows, (mask - 2) * length + offset, (ref[0], ref[1]))
        total = term if total is None else total + term
    return total


def far_kernel(step, offset, g_ref, left_ref, right_ref, acc_ref, out_ref):
    tile = row_block(out_ref.shape[0])
    rows = pl.ds(pl.multiple_of(pl.program_id(0) * tile, tile), tile)
    out_ref[rows] = acc_ref[rows] + far_terms(g_ref, rows, step, offset, left_ref, right_ref)


def far_product(g, left, right, acc, step, offset):
    _, depth, width = left.shape
    rows = g.shape[1]
    tile = row_block(rows)
    return pl.pallas_call(
        functools.partial(far_kernel, step, offset),
        grid=(rows // tile,),
        in_specs=[
            VMEM,
            VMEM,
            VMEM,
            VMEM,
        ],
        out_specs=VMEM,
        out_shape=pltpu.VMEM(acc.shape, F32),
        compiler_params=pltpu.CompilerParams(vmem_limit_bytes=LIMIT),
        cost_estimate=pl.CostEstimate(
            flops=2 * 8 * rows * depth * width, bytes_accessed=8 * rows * width, transcendentals=0
        ),
        name="far_product",
    )(g, left, right, acc)


def last_kernel(
    poles, step, offset, g_ref, left_ref, right_ref, acc_ref, own_ref, diag_ref, weight_ref, *rest
):
    out_refs, (y_ref, d_ref) = rest[:poles], rest[poles:]
    m = pl.program_id(0)
    tile, width = own_ref.shape[1:]
    count = tile // width
    blocks = y_ref.shape[0]
    rows = pl.ds(pl.multiple_of(m * tile, tile), tile)

    weight_real = weight_ref[0, 0]
    weight_imag = weight_ref[0, 1]
    total = acc_ref[rows] + far_terms(g_ref, rows, step, offset, left_ref, right_ref)
    real = -total[:, :width]
    imag = -total[:, width:]
    density = weight_real * imag + weight_imag * real
    other = weight_real * real - weight_imag * imag
    y_ref[pl.ds(m * count, count)] = density.reshape(count, poles, width // poles, width)

    def cross(lower, value):
        high = value.astype(BF16)
        low = (value - high.astype(F32)).astype(BF16)
        both = lax.dot_general(
            lower,
            jnp.concatenate([high, low], axis=1),
            (((0,), (0,)), ((), ())),
            preferred_element_type=F32,
        )
        return both[:, :width] + both[:, width:]

    part = (cross(own_ref[0], density) + cross(own_ref[1], other)).reshape(d_ref.shape)

    @pl.when(m == 0)
    def _():
        lead = (lax.axis_index("col") == 0).astype(F32)
        term = lead * (weight_real * diag_ref[1] + weight_imag * diag_ref[0])
        d_ref[...] = term.reshape(d_ref.shape) - part

    @pl.when(m > 0)
    def _():
        d_ref[...] -= part

    @pl.when(m == pl.num_programs(0) - 1)
    def _():
        for mask, out_ref in enumerate(out_refs):
            other_pole = lax.axis_index("pole") ^ mask
            kind = out_ref.dtype
            out_ref[:blocks] = y_ref[:, other_pole].astype(kind)
            out_ref[blocks] = d_ref[other_pole].astype(kind)


def last_product(g, left, right, acc, own, diag, weights, panel, step, offset, poles, kind):
    _, depth, width = left.shape
    rows = g.shape[1]
    tile = row_block(rows)
    blocks = rows // width
    shape = (blocks + 1, width // poles, width)
    return pl.pallas_call(
        functools.partial(last_kernel, poles, step, offset),
        grid=(rows // tile,),
        in_specs=[
            VMEM,
            VMEM,
            VMEM,
            VMEM,
            pl.BlockSpec((None, 2, tile, width), lambda m: (panel, 0, m, 0)),
            pl.BlockSpec((None, 2, width, width), lambda m: (panel, 0, 0, 0)),
            SMEM,
        ],
        out_specs=[VMEM] * poles,
        scratch_shapes=[
            pltpu.VMEM((blocks, poles, width // poles, width), F32),
            pltpu.VMEM((poles, width // poles, width), F32),
        ],
        out_shape=[pltpu.VMEM(shape, kind)] * poles,
        compiler_params=pltpu.CompilerParams(vmem_limit_bytes=LIMIT),
        cost_estimate=pl.CostEstimate(
            flops=2 * 8 * rows * depth * width, bytes_accessed=8 * rows * width, transcendentals=0
        ),
        name="last_product",
    )(g, left, right, acc, own, diag, weights)


def table_kernel(per_device, panels, cols, order_ref, supports_ref, counts_ref, send_ref, plan_ref):
    most, tiles = supports_ref.shape
    total = cols * per_device
    me = lax.axis_index("col")
    supports = supports_ref[...]
    counts = counts_ref[...]
    ids = lax.broadcasted_iota(jnp.int32, (total, tiles), 0)
    named = [(supports[k : k + 1] == ids) & (counts > k) for k in range(most)]
    any_named = named[0]
    for hit in named[1:]:
        any_named = any_named | hit
    tile_hits = jnp.where(any_named, 1.0, 0.0).astype(BF16)
    share = tiles // cols
    group_tile = lax.broadcasted_iota(jnp.int32, (tiles, cols), 0)
    group_col = lax.broadcasted_iota(jnp.int32, (tiles, cols), 1)
    group = (group_tile >= group_col * share) & (group_tile < (group_col + 1) * share)
    needed = jnp.minimum(
        jnp.dot(tile_hits, jnp.where(group, 1.0, 0.0).astype(BF16), preferred_element_type=F32), 1.0
    )
    first = lax.broadcasted_iota(jnp.int32, (total, total), 0)
    second = lax.broadcasted_iota(jnp.int32, (total, total), 1)
    earlier = (second <= first) & (first // per_device == second // per_device)
    rank = jnp.dot(
        jnp.where(earlier, 1.0, 0.0).astype(BF16), needed.astype(BF16), preferred_element_type=F32
    )
    block = lax.broadcasted_iota(jnp.int32, (total, cols), 0)
    dest = lax.broadcasted_iota(jnp.int32, (total, cols), 1)
    owner = block // per_device
    local = block - owner * per_device
    row = local // panels
    spot = local - row * panels
    panel = jnp.zeros_like(spot)
    for j in range(panels):
        panel = jnp.where(spot == j, order_ref[j], panel)
    code = (panel * (per_device // panels) + row).astype(F32)
    mine = (needed > 0.5) & (owner == me)
    for c in range(CAP):
        value = jnp.sum(jnp.where(mine & (rank == c + 1.0), code, 0.0), axis=0, keepdims=True)
        send_ref[c : c + 1] = value.astype(jnp.int32)
    lane = lax.broadcasted_iota(jnp.int32, (1, tiles), 1)
    order = jnp.zeros((1, tiles), jnp.int32)
    for j in range(panels):
        order = jnp.where(lane == j, order_ref[j], order)
    plan_ref[2 * most + 1 : 2 * most + 2] = order
    mask = (owner ^ me).astype(F32)
    spots = jnp.where((needed > 0.5) & (dest == me), mask * CAP + jnp.minimum(rank, CAP) - 1.0, 0.0)
    spots = jnp.sum(spots, axis=1, keepdims=True)
    for k, hit in enumerate(named):
        slot = jnp.sum(jnp.where(hit, spots, 0.0), axis=0, keepdims=True)
        plan_ref[k : k + 1] = slot.astype(jnp.int32)
    plan_ref[most : 2 * most] = lax.rem(supports, panels)
    plan_ref[2 * most : 2 * most + 1] = counts


def tables(supports, counts, order, cols, per_device, panels):
    tiles, most = supports.shape
    return pl.pallas_call(
        functools.partial(table_kernel, per_device, panels, cols),
        in_specs=[SMEM, VMEM, VMEM],
        out_specs=[VMEM] * 2,
        out_shape=[
            jax.ShapeDtypeStruct((CAP, cols), jnp.int32),
            jax.ShapeDtypeStruct((2 * most + 2, tiles), jnp.int32),
        ],
        compiler_params=pltpu.CompilerParams(vmem_limit_bytes=LIMIT),
        cost_estimate=pl.CostEstimate(flops=1 << 20, bytes_accessed=1 << 20, transcendentals=0),
        name="tables",
    )(order, supports.T, counts.reshape(1, tiles))


def total_of(parts, blocks):
    density = tree_sum([part[:blocks].astype(F32) for part in parts])
    return density.astype(BF16), tree_sum([part[blocks].astype(F32) for part in parts])


def settle_kernel(poles, blocks, *refs):
    density_ref, diag_ref = refs[-2:]
    for q in range(diag_ref.shape[0]):
        density, diag = total_of(refs[q * poles : (q + 1) * poles], blocks)
        density_ref[q * blocks : (q + 1) * blocks] = density
        diag_ref[q] = diag


def settle(groups, blocks):
    poles = len(groups[0])
    depth, width = groups[0][0].shape[1:]
    return pl.pallas_call(
        functools.partial(settle_kernel, poles, blocks),
        in_specs=[VMEM] * (poles * len(groups)),
        out_specs=[VMEM] * 2,
        out_shape=[
            jax.ShapeDtypeStruct((len(groups) * blocks, depth, width), BF16),
            jax.ShapeDtypeStruct((len(groups), depth, width), F32),
        ],
        compiler_params=pltpu.CompilerParams(vmem_limit_bytes=LIMIT),
        cost_estimate=pl.CostEstimate(flops=1 << 20, bytes_accessed=2 << 20, transcendentals=0),
        name="settle",
    )(*[part for group in groups for part in group])


def pick_kernel(poles, blocks, send_ref, early_ref, *rest):
    parts, out_refs, all_ref = rest[:poles], rest[poles:-1], rest[-1]
    early = early_ref.shape[0]
    me = lax.axis_index("col")
    all_ref[:early] = early_ref[...]
    density, diag = total_of(parts, blocks)
    all_ref[early:] = density
    for mask, out_ref in enumerate(out_refs):
        for c in range(CAP):
            out_ref[c] = all_ref[send_ref[c, me ^ mask]]
        out_ref[CAP] = diag.astype(BF16)


def pick(send, early, parts, blocks, cols):
    poles = len(parts)
    depth, width = early.shape[1:]
    return pl.pallas_call(
        functools.partial(pick_kernel, poles, blocks),
        in_specs=[SMEM] + [VMEM] * (1 + poles),
        out_specs=[VMEM] * cols,
        out_shape=[jax.ShapeDtypeStruct((CAP + 1, depth, width), BF16)] * cols,
        scratch_shapes=[pltpu.VMEM((early.shape[0] + blocks, depth, width), BF16)],
        compiler_params=pltpu.CompilerParams(vmem_limit_bytes=LIMIT),
        name="pick",
    )(send, early, *parts)


def near_join_kernel(diag_ref, *refs):
    parts, out_ref = refs[:-1], refs[-1]
    end = len(parts) * CAP
    for place, part in enumerate(parts):
        out_ref[place * CAP : (place + 1) * CAP] = part[:CAP]
    out_ref[end:] = diag_ref[...].astype(BF16)


def far_join_kernel(skip, *refs):
    parts, out_ref = refs[:-1], refs[-1]
    for place, part in enumerate(parts[skip:]):
        out_ref[place * CAP : (place + 1) * CAP] = part[:CAP]
    out_ref[out_ref.shape[0] - 1] = tree_sum([part[CAP].astype(F32) for part in parts]).astype(BF16)


def join(kernel, operands, slots):
    depth, width = operands[0].shape[1:]
    return pl.pallas_call(
        kernel,
        in_specs=[VMEM] * len(operands),
        out_specs=VMEM,
        out_shape=jax.ShapeDtypeStruct((slots, depth, width), BF16),
        compiler_params=pltpu.CompilerParams(vmem_limit_bytes=LIMIT),
    )(*operands)


def add_kernel(*refs):
    refs[-1][...] = tree_sum([ref[...] for ref in refs[:-1]])


def add(parts):
    return pl.pallas_call(
        add_kernel,
        in_specs=[VMEM] * len(parts),
        out_specs=VMEM,
        out_shape=jax.ShapeDtypeStruct(parts[0].shape, F32),
        compiler_params=pltpu.CompilerParams(vmem_limit_bytes=LIMIT),
        name="add",
    )(*parts)


def tile_kernel(plan_ref, row_ref, orbital_ref, core_hbm, *rest):
    poles = (len(rest) - 7) // 2
    near_parts, far_parts = rest[:poles], rest[poles : 2 * poles]
    valence_ref, potential_ref, diag_ref, blocks_ref, raw_ref, core_ref, core_sem = rest[-7:]
    tiles, most = row_ref.shape[:2]
    slots, poles, depth, width = blocks_ref.shape
    panels = diag_ref.shape[0]
    first = lax.axis_index("col") * tiles
    core_copy = pltpu.make_async_copy(core_hbm, core_ref, core_sem)
    core_copy.start()

    first_slots = 2 * CAP
    for mask, (near, far) in enumerate(zip(near_parts, far_parts)):
        owner = lax.axis_index("pole") ^ mask
        blocks_ref[:first_slots, owner] = near[:first_slots]
        blocks_ref[first_slots:, owner] = far[: slots - first_slots]
        raw_ref[: panels - 1, owner] = near[first_slots:]
        raw_ref[panels - 1, owner] = far[slots - first_slots]
    for j in range(panels):
        diag_ref[j] = raw_ref[plan_ref[2 * most + 1, j]].astype(F32)

    def one(t, _):
        valence = jnp.zeros((1, row_ref.shape[-1]), F32)
        for k in range(most):
            mixed = jnp.dot(
                blocks_ref[plan_ref[k, first + t]].reshape(poles * depth, width),
                orbital_ref[t, plan_ref[most + k, first + t]],
                preferred_element_type=F32,
            )
            term = jnp.sum(row_ref[t, k].astype(F32) * mixed, axis=0, keepdims=True)
            valence = valence + jnp.where(k < plan_ref[2 * most, first + t], term, 0.0)
        valence_ref[pl.ds(t, 1)] = valence
        return 0

    lax.fori_loop(0, tiles, one, 0, unroll=True)
    core_copy.wait()
    clamped = jnp.maximum(core_ref[...] + valence_ref[...], density_floor)
    potential_ref[...] = -exchange_coeff * clamped ** (1.0 / 3.0)


def tile_stage(plan, rows, orbitals, core, near_parts, far_parts, cols):
    _, _, width, _ = rows.shape
    panels = orbitals.shape[1]
    slots = cols * CAP
    poles = len(near_parts)
    depth = width // poles
    valence, potential, diag = pl.pallas_call(
        tile_kernel,
        in_specs=[SMEM, VMEM, VMEM, pl.BlockSpec(memory_space=pl.ANY)] + [VMEM] * (2 * poles),
        out_specs=[VMEM] * 3,
        out_shape=[
            jax.ShapeDtypeStruct(core.shape, F32),
            jax.ShapeDtypeStruct(core.shape, F32),
            jax.ShapeDtypeStruct((panels, poles, depth, width), F32),
        ],
        scratch_shapes=[
            pltpu.VMEM((slots, poles, depth, width), BF16),
            pltpu.VMEM((panels, poles, depth, width), BF16),
            pltpu.VMEM(core.shape, F32),
            pltpu.SemaphoreType.DMA(()),
        ],
        compiler_params=pltpu.CompilerParams(vmem_limit_bytes=LIMIT),
        name="tile_stage",
    )(plan, rows, orbitals, core, *near_parts, *far_parts)
    return valence, potential, diag.reshape(panels, width, width)


def body(
    inverse,
    panels,
    diag_inverse,
    pole_weights,
    supports,
    counts,
    panel_order,
    row_orbitals,
    panel_orbitals,
    core_density,
):
    cols = lax.axis_size("col")
    poles = lax.axis_size("pole")
    matrix = inverse[0]
    own = panels[0]
    diag = diag_inverse[0]
    panel_count, _, rows, width = own.shape
    blocks = rows // width
    per_device = blocks * panel_count
    steps = range(1, cols // 2)

    pieces = []
    for q in range(panel_count):
        cut = rows if q == 0 else rows // 2
        pieces += [(q, 0, cut)] + ([(q, cut, rows - cut)] if cut < rows else [])

    partner = swap(own, "col", 1)
    remote = {}
    for piece, (q, offset, depth) in enumerate(pieces):
        for step in steps:
            remote[step, piece] = swap(own[q, :, offset : offset + depth], "col", 2 * step)
    forward = {}
    for (step, piece), value in remote.items():
        forward[step, piece] = swap(value, "col", 1)

    send, plan = tables(supports, counts, panel_order, cols, per_device, panel_count)
    acc, staged = near_product(matrix, own, partner)
    sums = []
    for piece, (q, offset, depth) in enumerate(pieces):
        for step in steps:
            left, right = remote[step, piece], forward[step, piece]
            if step < cols // 2 - 1 or offset + depth < rows:
                acc[q] = far_product(staged, left, right, acc[q], step, offset)
                continue
            kind = F32 if q == 0 else BF16
            parts = last_product(
                staged, left, right, acc[q], own, diag, pole_weights, q, step, offset, poles, kind
            )
            group = [parts[0]]
            for mask in range(1, poles):
                group.append(swap(parts[mask], "pole", mask))
            sums.append(group)

    early, early_diag = settle(sums[:-1], blocks)
    spread = [early_diag]
    for mask in range(1, cols):
        spread.append(swap(early_diag, "col", mask))
    diag_rows = add(spread)
    messages = pick(send, early, sums[-1], blocks, cols)
    arrived = [messages[0]]
    for mask in range(1, cols):
        arrived.append(swap(messages[mask], "col", mask))
    panels_early = diag_rows.shape[0]
    near = join(near_join_kernel, [diag_rows] + arrived[:2], 2 * CAP + panels_early)
    gathered_near = [near]
    for mask in range(1, poles):
        gathered_near.append(swap(near, "pole", mask))
    far = join(functools.partial(far_join_kernel, 2), arrived, (cols - 2) * CAP + 1)
    gathered_far = [far]
    for mask in range(1, poles):
        gathered_far.append(swap(far, "pole", mask))
    return tile_stage(plan, row_orbitals, panel_orbitals, core_density, gathered_near, gathered_far, cols)


def solution(mesh):
    placed = (
        P(("job", "pole"), None, "col", None),
        P(("job", "pole"), None, None, "col", None),
        P(("job", "pole"), None, None, None, None),
        P(("job", "pole"), None),
        P(),
        P(),
        P(),
        P(("job", "col"), None, None, "pole"),
        P(("job", "col"), None, None, "pole"),
        P(("job", "col"), "pole"),
    )
    return jax.shard_map(
        body,
        mesh=mesh,
        in_specs=placed,
        out_specs=(P(("job", "col"), "pole"), P(("job", "col"), "pole"), P("job", None, None)),
        check_vma=False,
    )
```

```python
import functools

import jax
import jax.numpy as jnp
from jax import lax
from jax.experimental import pallas as pl
from jax.experimental.pallas import tpu as pltpu
from jax.sharding import PartitionSpec as P


CAP = 3

exchange_coeff = (3.0 / 3.141592653589793) ** (1.0 / 3.0)
density_floor = 0.5

F32 = jnp.float32
BF16 = jnp.bfloat16
SMEM = pl.BlockSpec(memory_space=pltpu.SMEM)
VMEM = pl.BlockSpec(memory_space=pltpu.VMEM)
LIMIT = 10 * 1024 * 1024
NEAR_LIMIT = 26 * 1024 * 1024


def swap(value, axis, mask):
    size = lax.axis_size(axis)
    return lax.ppermute(value, axis, [(i, i ^ mask) for i in range(size)])


def tree_sum(values):
    while len(values) > 1:
        values = [values[i] + values[i + 1] for i in range(0, len(values) - 1, 2)] + values[len(values) // 2 * 2 :]
    return values[0]


def row_block(rows):
    for size in (768, 512, 384, 256, 128):
        if rows % size == 0:
            return size
    return rows


def near_block(rows):
    return 384 if rows % 384 == 0 else row_block(rows)


def complex_product(g_ref, rows, start, lower):
    real, imag = lower
    columns = pl.ds(start, real.shape[0])
    first = jnp.dot(
        g_ref[0, rows, columns], jnp.concatenate([real, imag], axis=1), preferred_element_type=F32
    )
    second = jnp.dot(
        g_ref[1, rows, columns], jnp.concatenate([-imag, real], axis=1), preferred_element_type=F32
    )
    return first + second


def near_kernel(g_hbm, own_ref, partner_ref, *rest):
    acc_refs, (far_ref, near_ref, near_sem, far_sem) = rest[:-4], rest[-4:]
    length, order = g_hbm.shape[1:]
    cols = order // length
    tile = near_block(length)
    tiles = length // tile
    m = pl.program_id(0)
    me = lax.axis_index("col")
    starts = [pl.multiple_of((me ^ mask) * length, length) for mask in range(cols)]

    def near_copy(step, mask):
        rows = pl.ds(step * tile, tile)
        return pltpu.make_async_copy(
            g_hbm.at[:, rows, pl.ds(starts[mask], length)],
            near_ref.at[:, rows, pl.ds(mask * length, length)],
            near_sem.at[step, mask],
        )

    def far_copy(mask):
        return pltpu.make_async_copy(
            g_hbm.at[:, :, pl.ds(starts[mask], length)],
            far_ref.at[:, :, pl.ds((mask - 2) * length, length)],
            far_sem.at[mask - 2],
        )

    @pl.when(m == 0)
    def _():
        near_copy(0, 0).start()
        near_copy(0, 1).start()

    near_copy(m, 0).wait()

    @pl.when(m == 0)
    def _():
        for step in range(1, tiles):
            near_copy(step, 0).start()
            near_copy(step, 1).start()

    @pl.when(m == min(1, tiles - 1))
    def _():
        for mask in range(2, cols):
            far_copy(mask).start()

    near_copy(m, 1).wait()
    rows = pl.ds(pl.multiple_of(m * tile, tile), tile)
    for q, acc_ref in enumerate(acc_refs):
        acc_ref[rows] = complex_product(
            near_ref, rows, 0, (own_ref[q, 0], own_ref[q, 1])
        ) + complex_product(near_ref, rows, length, (partner_ref[q, 0], partner_ref[q, 1]))

    @pl.when(m == tiles - 1)
    def _():
        for mask in range(2, cols):
            far_copy(mask).wait()


def near_product(matrix, own, partner):
    panels, _, rows, width = own.shape
    order = matrix.shape[2]
    tile = near_block(rows)
    results = pl.pallas_call(
        near_kernel,
        grid=(rows // tile,),
        in_specs=[pl.BlockSpec(memory_space=pl.ANY), VMEM, VMEM],
        out_specs=[VMEM] * (panels + 1),
        out_shape=[pltpu.VMEM((rows, 2 * width), F32)] * panels
        + [pltpu.VMEM((2, rows, order - 2 * rows), BF16)],
        scratch_shapes=[
            pltpu.VMEM((2, rows, 2 * rows), BF16),
            pltpu.SemaphoreType.DMA((rows // tile, 2)),
            pltpu.SemaphoreType.DMA((order // rows - 2,)),
        ],
        compiler_params=pltpu.CompilerParams(vmem_limit_bytes=NEAR_LIMIT),
        cost_estimate=pl.CostEstimate(
            flops=2 * 8 * rows * rows * panels * width, bytes_accessed=4 * rows * order, transcendentals=0
        ),
    )(matrix, own, partner)
    return list(results[:-1]), results[-1]


def far_terms(g_ref, rows, step, offset, left_ref, right_ref):
    length = g_ref.shape[1]
    total = None
    for mask, ref in ((2 * step, left_ref), (2 * step + 1, right_ref)):
        term = complex_product(g_ref, rows, (mask - 2) * length + offset, (ref[0], ref[1]))
        total = term if total is None else total + term
    return total


def far_kernel(step, offset, g_ref, left_ref, right_ref, acc_ref, out_ref):
    tile = row_block(out_ref.shape[0])
    rows = pl.ds(pl.multiple_of(pl.program_id(0) * tile, tile), tile)
    out_ref[rows] = acc_ref[rows] + far_terms(g_ref, rows, step, offset, left_ref, right_ref)


def far_product(g, left, right, acc, step, offset):
    _, depth, width = left.shape
    rows = g.shape[1]
    tile = row_block(rows)
    return pl.pallas_call(
        functools.partial(far_kernel, step, offset),
        grid=(rows // tile,),
        in_specs=[
            VMEM,
            VMEM,
            VMEM,
            VMEM,
        ],
        out_specs=VMEM,
        out_shape=pltpu.VMEM(acc.shape, F32),
        compiler_params=pltpu.CompilerParams(vmem_limit_bytes=LIMIT),
        cost_estimate=pl.CostEstimate(
            flops=2 * 8 * rows * depth * width, bytes_accessed=8 * rows * width, transcendentals=0
        ),
    )(g, left, right, acc)


def last_kernel(
    poles, step, offset, g_ref, left_ref, right_ref, acc_ref, own_ref, diag_ref, weight_ref, *rest
):
    out_refs, (y_ref, d_ref) = rest[:poles], rest[poles:]
    m = pl.program_id(0)
    tile, width = own_ref.shape[1:]
    count = tile // width
    blocks = y_ref.shape[0]
    rows = pl.ds(pl.multiple_of(m * tile, tile), tile)

    weight_real = weight_ref[0, 0]
    weight_imag = weight_ref[0, 1]
    total = acc_ref[rows] + far_terms(g_ref, rows, step, offset, left_ref, right_ref)
    real = -total[:, :width]
    imag = -total[:, width:]
    density = weight_real * imag + weight_imag * real
    other = weight_real * real - weight_imag * imag
    y_ref[pl.ds(m * count, count)] = density.reshape(count, poles, width // poles, width)

    def cross(lower, value):
        high = value.astype(BF16)
        low = (value - high.astype(F32)).astype(BF16)
        both = lax.dot_general(
            lower,
            jnp.concatenate([high, low], axis=1),
            (((0,), (0,)), ((), ())),
            preferred_element_type=F32,
        )
        return both[:, :width] + both[:, width:]

    lower = jnp.concatenate([own_ref[0], own_ref[1]], axis=0)
    part = cross(lower, jnp.concatenate([density, other], axis=0)).reshape(d_ref.shape)

    @pl.when(m == 0)
    def _():
        lead = (lax.axis_index("col") == 0).astype(F32)
        term = lead * (weight_real * diag_ref[1] + weight_imag * diag_ref[0])
        d_ref[...] = term.reshape(d_ref.shape) - part

    @pl.when(m > 0)
    def _():
        d_ref[...] -= part

    @pl.when(m == pl.num_programs(0) - 1)
    def _():
        for mask, out_ref in enumerate(out_refs):
            other_pole = lax.axis_index("pole") ^ mask
            kind = out_ref.dtype
            out_ref[:blocks] = y_ref[:, other_pole].astype(kind)
            out_ref[blocks] = d_ref[other_pole].astype(kind)


def last_product(g, left, right, acc, own, diag, weights, panel, step, offset, poles, kind):
    _, depth, width = left.shape
    rows = g.shape[1]
    tile = row_block(rows)
    blocks = rows // width
    shape = (blocks + 1, width // poles, width)
    return pl.pallas_call(
        functools.partial(last_kernel, poles, step, offset),
        grid=(rows // tile,),
        in_specs=[
            VMEM,
            VMEM,
            VMEM,
            VMEM,
            pl.BlockSpec((None, 2, tile, width), lambda m: (panel, 0, m, 0)),
            pl.BlockSpec((None, 2, width, width), lambda m: (panel, 0, 0, 0)),
            SMEM,
        ],
        out_specs=[VMEM] * poles,
        scratch_shapes=[
            pltpu.VMEM((blocks, poles, width // poles, width), F32),
            pltpu.VMEM((poles, width // poles, width), F32),
        ],
        out_shape=[pltpu.VMEM(shape, kind)] * poles,
        compiler_params=pltpu.CompilerParams(vmem_limit_bytes=LIMIT),
        cost_estimate=pl.CostEstimate(
            flops=2 * 8 * rows * depth * width, bytes_accessed=8 * rows * width, transcendentals=0
        ),
    )(g, left, right, acc, own, diag, weights)


def table_kernel(per_device, panels, cols, order_ref, supports_ref, counts_ref, send_ref, plan_ref):
    most, tiles = supports_ref.shape
    total = cols * per_device
    me = lax.axis_index("col")
    supports = supports_ref[...]
    counts = counts_ref[...]
    ids = lax.broadcasted_iota(jnp.int32, (total, tiles), 0)
    named = [(supports[k : k + 1] == ids) & (counts > k) for k in range(most)]
    any_named = named[0]
    for hit in named[1:]:
        any_named = any_named | hit
    tile_hits = jnp.where(any_named, 1.0, 0.0).astype(BF16)
    share = tiles // cols
    group_tile = lax.broadcasted_iota(jnp.int32, (tiles, cols), 0)
    group_col = lax.broadcasted_iota(jnp.int32, (tiles, cols), 1)
    group = (group_tile >= group_col * share) & (group_tile < (group_col + 1) * share)
    needed = jnp.minimum(
        jnp.dot(tile_hits, jnp.where(group, 1.0, 0.0).astype(BF16), preferred_element_type=F32), 1.0
    )
    first = lax.broadcasted_iota(jnp.int32, (total, total), 0)
    second = lax.broadcasted_iota(jnp.int32, (total, total), 1)
    earlier = (second <= first) & (first // per_device == second // per_device)
    rank = jnp.dot(
        jnp.where(earlier, 1.0, 0.0).astype(BF16), needed.astype(BF16), preferred_element_type=F32
    )
    block = lax.broadcasted_iota(jnp.int32, (total, cols), 0)
    dest = lax.broadcasted_iota(jnp.int32, (total, cols), 1)
    owner = block // per_device
    local = block - owner * per_device
    row = local // panels
    spot = local - row * panels
    panel = jnp.zeros_like(spot)
    for j in range(panels):
        panel = jnp.where(spot == j, order_ref[j], panel)
    code = (panel * (per_device // panels) + row).astype(F32)
    mine = (needed > 0.5) & (owner == me)
    for c in range(CAP):
        value = jnp.sum(jnp.where(mine & (rank == c + 1.0), code, 0.0), axis=0, keepdims=True)
        send_ref[c : c + 1] = value.astype(jnp.int32)
    lane = lax.broadcasted_iota(jnp.int32, (1, tiles), 1)
    order = jnp.zeros((1, tiles), jnp.int32)
    for j in range(panels):
        order = jnp.where(lane == j, order_ref[j], order)
    plan_ref[2 * most + 1 : 2 * most + 2] = order
    mask = (owner ^ me).astype(F32)
    spots = jnp.where((needed > 0.5) & (dest == me), mask * CAP + jnp.minimum(rank, CAP) - 1.0, 0.0)
    spots = jnp.sum(spots, axis=1, keepdims=True)
    for k, hit in enumerate(named):
        slot = jnp.sum(jnp.where(hit, spots, 0.0), axis=0, keepdims=True)
        plan_ref[k : k + 1] = slot.astype(jnp.int32)
    plan_ref[most : 2 * most] = lax.rem(supports, panels)
    plan_ref[2 * most : 2 * most + 1] = counts


def tables(supports, counts, order, cols, per_device, panels):
    tiles, most = supports.shape
    return pl.pallas_call(
        functools.partial(table_kernel, per_device, panels, cols),
        in_specs=[SMEM, VMEM, VMEM],
        out_specs=[VMEM] * 2,
        out_shape=[
            jax.ShapeDtypeStruct((CAP, cols), jnp.int32),
            jax.ShapeDtypeStruct((2 * most + 2, tiles), jnp.int32),
        ],
        compiler_params=pltpu.CompilerParams(vmem_limit_bytes=LIMIT),
        cost_estimate=pl.CostEstimate(flops=1 << 20, bytes_accessed=1 << 20, transcendentals=0),
    )(order, supports.T, counts.reshape(1, tiles))


def total_of(parts, blocks):
    density = tree_sum([part[:blocks].astype(F32) for part in parts])
    return density.astype(BF16), tree_sum([part[blocks].astype(F32) for part in parts])


def settle_kernel(poles, blocks, *refs):
    density_ref, diag_ref = refs[-2:]
    for q in range(diag_ref.shape[0]):
        density, diag = total_of(refs[q * poles : (q + 1) * poles], blocks)
        density_ref[q * blocks : (q + 1) * blocks] = density
        diag_ref[q] = diag


def settle(groups, blocks):
    poles = len(groups[0])
    depth, width = groups[0][0].shape[1:]
    return pl.pallas_call(
        functools.partial(settle_kernel, poles, blocks),
        in_specs=[VMEM] * (poles * len(groups)),
        out_specs=[VMEM] * 2,
        out_shape=[
            jax.ShapeDtypeStruct((len(groups) * blocks, depth, width), BF16),
            jax.ShapeDtypeStruct((len(groups), depth, width), F32),
        ],
        compiler_params=pltpu.CompilerParams(vmem_limit_bytes=LIMIT),
        cost_estimate=pl.CostEstimate(flops=1 << 20, bytes_accessed=2 << 20, transcendentals=0),
    )(*[part for group in groups for part in group])


def pick_kernel(poles, blocks, send_ref, early_ref, *rest):
    parts, out_refs, all_ref = rest[:poles], rest[poles:-1], rest[-1]
    early = early_ref.shape[0]
    me = lax.axis_index("col")
    all_ref[:early] = early_ref[...]
    density, diag = total_of(parts, blocks)
    all_ref[early:] = density
    for mask, out_ref in enumerate(out_refs):
        for c in range(CAP):
            out_ref[c] = all_ref[send_ref[c, me ^ mask]]
        out_ref[CAP] = diag.astype(BF16)


def pick(send, early, parts, blocks, cols):
    poles = len(parts)
    depth, width = early.shape[1:]
    return pl.pallas_call(
        functools.partial(pick_kernel, poles, blocks),
        in_specs=[SMEM] + [VMEM] * (1 + poles),
        out_specs=[VMEM] * cols,
        out_shape=[jax.ShapeDtypeStruct((CAP + 1, depth, width), BF16)] * cols,
        scratch_shapes=[pltpu.VMEM((early.shape[0] + blocks, depth, width), BF16)],
        compiler_params=pltpu.CompilerParams(vmem_limit_bytes=LIMIT),
    )(send, early, *parts)


def near_join_kernel(diag_ref, *refs):
    parts, out_ref = refs[:-1], refs[-1]
    end = len(parts) * CAP
    for place, part in enumerate(parts):
        out_ref[place * CAP : (place + 1) * CAP] = part[:CAP]
    out_ref[end:] = diag_ref[...].astype(BF16)


def far_join_kernel(skip, *refs):
    parts, out_ref = refs[:-1], refs[-1]
    for place, part in enumerate(parts[skip:]):
        out_ref[place * CAP : (place + 1) * CAP] = part[:CAP]
    out_ref[out_ref.shape[0] - 1] = tree_sum([part[CAP].astype(F32) for part in parts]).astype(BF16)


def join(kernel, operands, slots):
    depth, width = operands[0].shape[1:]
    return pl.pallas_call(
        kernel,
        in_specs=[VMEM] * len(operands),
        out_specs=VMEM,
        out_shape=jax.ShapeDtypeStruct((slots, depth, width), BF16),
        compiler_params=pltpu.CompilerParams(vmem_limit_bytes=LIMIT),
    )(*operands)


def add_kernel(*refs):
    refs[-1][...] = tree_sum([ref[...] for ref in refs[:-1]])


def add(parts):
    return pl.pallas_call(
        add_kernel,
        in_specs=[VMEM] * len(parts),
        out_specs=VMEM,
        out_shape=jax.ShapeDtypeStruct(parts[0].shape, F32),
        compiler_params=pltpu.CompilerParams(vmem_limit_bytes=LIMIT),
    )(*parts)


def tile_kernel(plan_ref, row_ref, orbital_ref, core_hbm, *rest):
    poles = (len(rest) - 7) // 2
    near_parts, far_parts = rest[:poles], rest[poles : 2 * poles]
    valence_ref, potential_ref, diag_ref, blocks_ref, raw_ref, core_ref, core_sem = rest[-7:]
    tiles, most = row_ref.shape[:2]
    slots, poles, depth, width = blocks_ref.shape
    panels = diag_ref.shape[0]
    first = lax.axis_index("col") * tiles
    core_copy = pltpu.make_async_copy(core_hbm, core_ref, core_sem)
    core_copy.start()

    first_slots = 2 * CAP
    for mask, (near, far) in enumerate(zip(near_parts, far_parts)):
        owner = lax.axis_index("pole") ^ mask
        blocks_ref[:first_slots, owner] = near[:first_slots]
        blocks_ref[first_slots:, owner] = far[: slots - first_slots]
        raw_ref[: panels - 1, owner] = near[first_slots:]
        raw_ref[panels - 1, owner] = far[slots - first_slots]
    for j in range(panels):
        diag_ref[j] = raw_ref[plan_ref[2 * most + 1, j]].astype(F32)

    def one(t, _):
        valence = jnp.zeros((1, row_ref.shape[-1]), F32)
        for k in range(most):
            mixed = jnp.dot(
                blocks_ref[plan_ref[k, first + t]].reshape(poles * depth, width),
                orbital_ref[t, plan_ref[most + k, first + t]],
                preferred_element_type=F32,
            )
            term = jnp.sum(row_ref[t, k].astype(F32) * mixed, axis=0, keepdims=True)
            valence = valence + jnp.where(k < plan_ref[2 * most, first + t], term, 0.0)
        valence_ref[pl.ds(t, 1)] = valence
        return 0

    lax.fori_loop(0, tiles, one, 0, unroll=True)
    core_copy.wait()
    clamped = jnp.maximum(core_ref[...] + valence_ref[...], density_floor)
    potential_ref[...] = -exchange_coeff * clamped ** (1.0 / 3.0)


def tile_stage(plan, rows, orbitals, core, near_parts, far_parts, cols):
    _, _, width, _ = rows.shape
    panels = orbitals.shape[1]
    slots = cols * CAP
    poles = len(near_parts)
    depth = width // poles
    valence, potential, diag = pl.pallas_call(
        tile_kernel,
        in_specs=[SMEM, VMEM, VMEM, pl.BlockSpec(memory_space=pl.ANY)] + [VMEM] * (2 * poles),
        out_specs=[VMEM] * 3,
        out_shape=[
            jax.ShapeDtypeStruct(core.shape, F32),
            jax.ShapeDtypeStruct(core.shape, F32),
            jax.ShapeDtypeStruct((panels, poles, depth, width), F32),
        ],
        scratch_shapes=[
            pltpu.VMEM((slots, poles, depth, width), BF16),
            pltpu.VMEM((panels, poles, depth, width), BF16),
            pltpu.VMEM(core.shape, F32),
            pltpu.SemaphoreType.DMA(()),
        ],
        compiler_params=pltpu.CompilerParams(vmem_limit_bytes=LIMIT),
    )(plan, rows, orbitals, core, *near_parts, *far_parts)
    return valence, potential, diag.reshape(panels, width, width)


def body(
    inverse,
    panels,
    diag_inverse,
    pole_weights,
    supports,
    counts,
    panel_order,
    row_orbitals,
    panel_orbitals,
    core_density,
):
    cols = lax.axis_size("col")
    poles = lax.axis_size("pole")
    matrix = inverse[0]
    own = panels[0]
    diag = diag_inverse[0]
    panel_count, _, rows, width = own.shape
    blocks = rows // width
    per_device = blocks * panel_count
    steps = range(1, cols // 2)

    pieces = []
    for q in range(panel_count):
        cut = rows if q == 0 else rows // 2
        pieces += [(q, 0, cut)] + ([(q, cut, rows - cut)] if cut < rows else [])

    partner = swap(own, "col", 1)
    remote = {}
    for piece, (q, offset, depth) in enumerate(pieces):
        for step in steps:
            remote[step, piece] = swap(own[q, :, offset : offset + depth], "col", 2 * step)
    forward = {}
    for (step, piece), value in remote.items():
        forward[step, piece] = swap(value, "col", 1)

    send, plan = tables(supports, counts, panel_order, cols, per_device, panel_count)
    acc, staged = near_product(matrix, own, partner)
    sums = []
    for piece, (q, offset, depth) in enumerate(pieces):
        for step in steps:
            left, right = remote[step, piece], forward[step, piece]
            if step < cols // 2 - 1 or offset + depth < rows:
                acc[q] = far_product(staged, left, right, acc[q], step, offset)
                continue
            kind = F32 if q == 0 else BF16
            parts = last_product(
                staged, left, right, acc[q], own, diag, pole_weights, q, step, offset, poles, kind
            )
            group = [parts[0]]
            for mask in range(1, poles):
                group.append(swap(parts[mask], "pole", mask))
            sums.append(group)

    early, early_diag = settle(sums[:-1], blocks)
    spread = [early_diag]
    for mask in range(1, cols):
        spread.append(swap(early_diag, "col", mask))
    diag_rows = add(spread)
    messages = pick(send, early, sums[-1], blocks, cols)
    arrived = [messages[0]]
    for mask in range(1, cols):
        arrived.append(swap(messages[mask], "col", mask))
    panels_early = diag_rows.shape[0]
    near = join(near_join_kernel, [diag_rows] + arrived[:2], 2 * CAP + panels_early)
    gathered_near = [near]
    for mask in range(1, poles):
        gathered_near.append(swap(near, "pole", mask))
    far = join(functools.partial(far_join_kernel, 2), arrived, (cols - 2) * CAP + 1)
    gathered_far = [far]
    for mask in range(1, poles):
        gathered_far.append(swap(far, "pole", mask))
    return tile_stage(plan, row_orbitals, panel_orbitals, core_density, gathered_near, gathered_far, cols)


def solution(mesh):
    placed = (
        P(("job", "pole"), None, "col", None),
        P(("job", "pole"), None, None, "col", None),
        P(("job", "pole"), None, None, None, None),
        P(("job", "pole"), None),
        P(),
        P(),
        P(),
        P(("job", "col"), None, None, "pole"),
        P(("job", "col"), None, None, "pole"),
        P(("job", "col"), "pole"),
    )
    return jax.shard_map(
        body,
        mesh=mesh,
        in_specs=placed,
        out_specs=(P(("job", "col"), "pole"), P(("job", "col"), "pole"), P("job", None, None)),
        check_vma=False,
    )
```
